32 devices in a mesh: fsdp: 4 (over z), lat: 8 (over y, x, core).
Axes of the slice: x: 2, y: 2, z: 4, core: 2. Of those that a mesh axis runs over, the one named last changes fastest.
Arguments:
- fields: bfloat16 [4, 128, 360, 192], P('fsdp', 'lat'), may hold values from -6 to 6
- cotangent: bfloat16 [4, 128, 360, 192], P('fsdp', 'lat'), may hold values from -6 to 6
- kernel_one: bfloat16 [3, 3, 192, 192], P(None, None, None, 'fsdp'), may hold values from -0.15625 to 0.15625
- kernel_two: bfloat16 [3, 3, 192, 192], P(None, None, None, 'fsdp'), may hold values from -0.15625 to 0.15625
Outputs:
- block_out: bfloat16 [4, 128, 360, 192], P('fsdp', 'lat')
- field_grad: bfloat16 [4, 128, 360, 192], P('fsdp', 'lat')
- grad_one: float32 [3, 3, 192, 192], P(None, None, None, 'fsdp')
- grad_two: float32 [3, 3, 192, 192], P(None, None, None, 'fsdp')
The draws below stay inside these ranges and needn't reach their ends.
All inputs are finite; a program needn't handle non-finite values.
Results may differ from the reference program's by a relative error of at most 0.0033.
Values may be sent and summed in bfloat16 or wider, within the bound.
No kernel may reach another device: no remote copies, remote signals or barrier semaphores. Data moves between devices by JAX's collectives and lax.ppermute only.
A program may use at most 128 MiB of HBM per device.

```python
import jax
import jax.numpy as jnp
from jax import lax

C = 192
LON = 360
LAT = 128
BATCH = 4


def with_spikes(drawn, key, source, target, parts, factor):
    def block_of(axis_at):
        return (jnp.arange(drawn.shape[axis_at]) // (drawn.shape[axis_at] // parts)).reshape((-1,) + (1,) * (drawn.ndim - 1 - axis_at))

    first = jax.random.permutation(key, parts)[block_of(target)]
    other_side = (block_of(target) + parts // 2) % parts
    return jnp.where((block_of(source) == first) | (block_of(source) == other_side), factor * drawn, drawn)


def block_levels(stream_key, extent, cuts, least, top_value):
    gain = 1.0
    for dim, shards_of in cuts:
        draws = jax.random.uniform(jax.random.fold_in(jax.random.fold_in(stream_key, 6), dim), (shards_of,), jnp.float32, least / len(cuts), top_value / len(cuts))
        gain = gain * jnp.repeat(jnp.exp(draws), extent[dim] // shards_of).reshape((-1,) + (1,) * (len(extent) - 1 - dim))
    return gain


def scatter_about(rng, dims, deviation, bound, cuts=(), held_as=jnp.bfloat16):
    values = jax.random.normal(rng, dims, jnp.float32) * deviation
    if len(cuts) > 0:
        values = block_levels(rng, dims, cuts, -0.22, 0.18) * values
    return jnp.clip(values, min=-bound, max=bound).astype(held_as)


def heavy_noise(stream_key, dims, width, most, cuts, heavy, held_as=jnp.bfloat16):
    entries = width * jax.random.normal(stream_key, dims, jnp.float32)
    if cuts:
        entries = entries * block_levels(stream_key, dims, cuts, -0.22, 0.18)
    return jnp.clip(with_spikes(entries, jax.random.fold_in(stream_key, 3), *heavy), -most, most).astype(held_as)


def setup_inputs(seed: int = 0) -> dict:
    key_of = jax.random.split(jax.random.key(seed), 5)
    return {
        "fields": scatter_about(key_of[0], (BATCH, LAT, LON, C), 1.0, 6.0, ((0, 4), (1, 8))),
        "cotangent": heavy_noise(key_of[1], (BATCH, LAT, LON, C), 1.0, 6.0, ((0, 4), (1, 8)), (0, 3, 4, 2.0)),
        "kernel_one": scatter_about(key_of[2], (3, 3, C, C), (9 * C) ** -0.5, 0.15625, ((3, 4),)),
        "kernel_two": scatter_about(key_of[3], (3, 3, C, C), (9 * C) ** -0.5, 0.15625, ((3, 4),)),
    }


def wrap_longitude(values):
    return jnp.concatenate([values[:, :, -2:], values, values[:, :, :2]], axis=2)

def padded_rows(values):
    return wrap_longitude(jnp.pad(values, ((0, 0), (2, 2), (0, 0), (0, 0))))

def correlate(padded, kernel):
    return lax.conv_general_dilated(padded.astype(jnp.float32), kernel.astype(jnp.float32), (1, 1), 'VALID', rhs_dilation=(2, 2), dimension_numbers=('NHWC', 'HWIO', 'NHWC'), precision=lax.Precision.HIGHEST)

def adjoint_kernel(kernel):
    return jnp.transpose(kernel[::-1, ::-1], (0, 1, 3, 2))

def normal_cdf(values):
    return 0.5 * (1.0 + jax.scipy.special.erf(values * 0.7071067811865476))

def kernel_terms(padded, grad_field, height, width_cells):
    grad_wide = grad_field.astype(jnp.float32)
    padded_wide = padded.astype(jnp.float32)
    return jnp.stack([jnp.stack([jnp.einsum('nhwc,nhwd->cd', padded_wide[:, 2 * a:2 * a + height, 2 * b:2 * b + width_cells], grad_wide, precision=lax.Precision.HIGHEST) for b in range(3)]) for a in range(3)])

def reference(fields, cotangent, kernel_one, kernel_two):
    height = fields.shape[1]
    width_cells = fields.shape[2]
    factor = 1.0 / jnp.sqrt(jnp.float32(fields.shape[0] * height * width_cells))

    def sample_work(pair):
        source, upstream = pair
        source = source[None]
        upstream = upstream[None]
        source_pad = padded_rows(source)
        preact = correlate(source_pad, kernel_one)
        hidden = (preact * normal_cdf(preact)).astype(jnp.bfloat16)
        hidden_pad = padded_rows(hidden)
        block_out = (source.astype(jnp.float32) + correlate(hidden_pad, kernel_two)).astype(jnp.bfloat16)
        back = correlate(padded_rows(upstream), adjoint_kernel(kernel_two))
        slope = normal_cdf(preact) + preact * jnp.exp(-0.5 * preact * preact) * 0.3989422804014327
        inner_grad = (back * slope).astype(jnp.bfloat16)
        field_grad = (upstream.astype(jnp.float32) + correlate(padded_rows(inner_grad), adjoint_kernel(kernel_one))).astype(jnp.bfloat16)
        grad_two = kernel_terms(hidden_pad, upstream, height, width_cells)
        grad_one = kernel_terms(source_pad, inner_grad, height, width_cells)
        return (block_out[0], field_grad[0], grad_one, grad_two)
    outputs, grads_in, ones, twos = lax.map(sample_work, (fields, cotangent))
    return (outputs, grads_in, lax.optimization_barrier(jnp.sum(ones, axis=0)) * factor, lax.optimization_barrier(jnp.sum(twos, axis=0)) * factor)
```

```python
import functools

import jax
import jax.numpy as jnp
from jax import lax
from jax.experimental import pallas as pl
from jax.experimental.pallas import tpu as pltpu
from jax.sharding import PartitionSpec as P

BF16 = jnp.bfloat16
F32 = jnp.float32
VMEM = pl.BlockSpec(memory_space=pltpu.VMEM)
SMEM = pl.BlockSpec(memory_space=pltpu.SMEM)
TAPS = 9
SLABS = 3 * TAPS
HALF = (SLABS + 1) // 2
LANES = 128


def call(body, name, out, specs, args, scratch=(), limit=40, flops=0, nbytes=0):
    return pl.pallas_call(
        body,
        name=name,
        out_shape=out,
        in_specs=specs,
        out_specs=jax.tree.map(lambda _: VMEM, out),
        scratch_shapes=list(scratch),
        compiler_params=pltpu.CompilerParams(vmem_limit_bytes=limit << 20),
        cost_estimate=pl.CostEstimate(flops=flops, bytes_accessed=nbytes, transcendentals=0),
    )(*args)


def padded_lanes(chan):
    return -(-chan // LANES) * LANES


def pack_body(parity, one, two, half):
    def slab(s):
        tap = s % TAPS
        if s < TAPS:
            return one[tap][:, :LANES]
        if s < 2 * TAPS:
            return two[tap][:, :LANES]
        return jnp.concatenate([one[tap][:, LANES:], two[tap][:, LANES:]], axis=1)

    for side in range(2):

        @pl.when(parity[0] == side)
        def _():
            for i in range(HALF):
                half[i] = slab(min(side * HALF + i, SLABS - 1))


def weights_body(parity, own, other, w1, w2, a1, a2):
    c = w1.shape[0]
    mine = parity[0] == 0

    def slab(s):
        side, i = divmod(s, HALF)
        first, second = (own, other) if side == 0 else (other, own)
        parts = [jnp.where(mine, first[f, i], second[f, i]) for f in range(own.shape[0])]
        return jnp.concatenate(parts, axis=0)

    for tap in range(TAPS):
        tails = slab(2 * TAPS + tap)
        rest = c - LANES
        one = jnp.concatenate([slab(tap), tails[:, :rest]], axis=1)
        two = jnp.concatenate([slab(TAPS + tap), tails[:, rest:]], axis=1)
        at = pl.ds(tap * c, c)
        back = pl.ds((TAPS - 1 - tap) * c, c)
        w1[:, at] = one
        w2[:, at] = two
        a1[:, back] = one.T
        a2[:, back] = two.T


def shifted(row, pad):
    lon = row.shape[1]
    fill = jnp.zeros((row.shape[0], pad), row.dtype)
    return (
        jnp.concatenate([row[:, lon - 2 :], row[:, : lon - 2], fill], axis=1),
        jnp.concatenate([row, fill], axis=1),
        jnp.concatenate([row[:, 2:], row[:, :2], fill], axis=1),
    )


def store_row(columns, at, row, pad):
    c = row.shape[0]
    for b, piece in enumerate(shifted(row, pad)):
        columns[at, b * c : (b + 1) * c] = piece


def taps_of(columns, at):
    return jnp.concatenate([columns[at], columns[at + 2], columns[at + 4]], axis=0)


def rows_of(columns, at, step):
    return jnp.concatenate([taps_of(columns, at + s) for s in range(step)], axis=1)


def normal_cdf(values):
    return 0.5 * (1.0 + lax.erf(values * 0.7071067811865476))


def first_body(step, fields, cot, above, below, w1, a2, fcol, ccol, hid, inn, up, down):
    height, c, lon = fields.shape
    wide = fcol.shape[2]
    pad = wide - lon
    for columns, source, base in ((fcol, fields, 0), (ccol, cot, 2)):
        for r in range(2):
            store_row(columns, r, above[base + r], pad)
            store_row(columns, height + 2 + r, below[base + r], pad)

        def fill(i, carry):
            store_row(columns, i + 2, source[i], pad)
            return carry

        lax.fori_loop(0, height, fill, 0)

    def work(t, carry):
        i = t * step
        pre = jnp.dot(w1[...], rows_of(fcol, i, step), preferred_element_type=F32)
        back = jnp.dot(a2[...], rows_of(ccol, i, step), preferred_element_type=F32)
        cdf = normal_cdf(pre)
        hidden = (pre * cdf).astype(BF16)
        slope = cdf + pre * jnp.exp(-0.5 * pre * pre) * 0.3989422804014327
        inner = (back * slope).astype(BF16)
        for s in range(step):
            hid[i + s] = hidden[:, s * wide : (s + 1) * wide]
            inn[i + s] = inner[:, s * wide : (s + 1) * wide]
        return carry

    lax.fori_loop(0, height // step, work, 0)
    for r in range(2):
        up[r] = hid[r][:, :lon]
        up[2 + r] = inn[r][:, :lon]
        down[r] = hid[height - 2 + r][:, :lon]
        down[2 + r] = inn[height - 2 + r][:, :lon]


def terms_body(step, scale, shards, fcol, ccol, hid, inn, out, g1, g2):
    height = hid.shape[0]
    c = hid.shape[1]
    g1[...] = jnp.zeros_like(g1)
    g2[...] = jnp.zeros_like(g2)
    contract = (((1,), (1,)), ((), ()))

    def work(t, carry):
        i = t * step
        for total, columns, field in ((g1, fcol, inn), (g2, ccol, hid)):
            rhs = jnp.concatenate([field[i + s] for s in range(step)], axis=1)
            total[...] += lax.dot_general(
                rows_of(columns, i, step), rhs, contract, preferred_element_type=F32
            )
        return carry

    lax.fori_loop(0, height // step, work, 0)
    share = c // shards
    depth = out.shape[3]

    def place(slab, value):
        for f in range(shards):
            start = slab * share
            while start < (slab + 1) * share:
                chunk, inside = divmod(start, depth)
                stop = min((slab + 1) * share, (chunk + 1) * depth)
                src = f * share + start - slab * share
                out[chunk % 2, chunk // 2, f, inside : inside + stop - start] = value[
                    src : src + stop - start
                ].astype(out.dtype)
                start = stop

    for tap in range(TAPS):
        one = g1[tap * c : (tap + 1) * c].T * scale
        two = g2[(TAPS - 1 - tap) * c : (TAPS - tap) * c] * scale
        place(tap, one[:, :LANES])
        place(TAPS + tap, two[:, :LANES])
        place(2 * TAPS + tap, jnp.concatenate([one[:, LANES:], two[:, LANES:]], axis=1))


def second_body(step, fields, cot, hid, inn, above, below, w2, a1, out, grad, columns):
    height, c, lon = fields.shape
    wide = columns.shape[2]
    pad = wide - lon
    for base, mid, weight, residual, result in (
        (0, hid, w2, fields, out),
        (2, inn, a1, cot, grad),
    ):
        for r in range(2):
            store_row(columns, r, above[base + r], pad)
            store_row(columns, height + 2 + r, below[base + r], pad)

        def fill(i, carry):
            store_row(columns, i + 2, mid[i][:, :lon], pad)
            return carry

        lax.fori_loop(0, height, fill, 0)

        def work(t, carry):
            i = t * step
            value = jnp.dot(weight[...], rows_of(columns, i, step), preferred_element_type=F32)
            for s in range(step):
                part = value[:, s * wide : s * wide + lon]
                result[i + s] = (residual[i + s].astype(F32) + part).astype(BF16)
            return carry

        lax.fori_loop(0, height // step, work, 0)


def unpack_body(share, chunks, one, two):
    count, depth, _ = chunks.shape
    c = one.shape[2]
    rest = c - LANES

    def rows(slab):
        parts = []
        start = slab * share
        while start < (slab + 1) * share:
            chunk, inside = divmod(start, depth)
            stop = min((slab + 1) * share, (chunk + 1) * depth)
            parts.append(chunks[chunk, inside : inside + stop - start])
            start = stop
        return parts[0] if len(parts) == 1 else jnp.concatenate(parts, axis=0)

    for tap in range(TAPS):
        tails = rows(2 * TAPS + tap)
        one[tap] = jnp.concatenate([rows(tap), tails[:, :rest]], axis=1)
        two[tap] = jnp.concatenate([rows(TAPS + tap), tails[:, rest:]], axis=1)


def shape(dims, dtype):
    return jax.ShapeDtypeStruct(dims, dtype)


def per_device(fields, cotangent, kernel_one, kernel_two):
    _, height, lon, c = fields.shape
    share = kernel_one.shape[3]
    shards = lax.axis_size("fsdp")
    bands = lax.axis_size("lat")
    wide = padded_lanes(lon)
    step = 4
    scale = 1.0 / (shards * fields.shape[0] * bands * height * lon) ** 0.5
    source = jnp.swapaxes(fields[0], 1, 2)
    upstream = jnp.swapaxes(cotangent[0], 1, 2)
    small = [
        jnp.swapaxes(k.reshape(TAPS, c, share), 1, 2) for k in (kernel_one, kernel_two)
    ]
    parity = (lax.axis_index("lat") % 2).astype(jnp.int32).reshape(1)
    forward = [(i, i + 1) for i in range(bands - 1)]
    backward = [(i + 1, i) for i in range(bands - 1)]
    swap = [(i, i ^ 1) for i in range(bands)]

    def edges(top, bottom):
        return lax.ppermute(bottom, "lat", forward), lax.ppermute(top, "lat", backward)

    above, below = edges(
        jnp.concatenate([source[:2], upstream[:2]], axis=0),
        jnp.concatenate([source[-2:], upstream[-2:]], axis=0),
    )
    half = call(
        pack_body, "pack", shape((HALF, share, LANES), BF16), [SMEM, VMEM, VMEM], (parity, *small)
    )
    own = lax.all_gather(half, "fsdp", axis=0)
    other = lax.ppermute(own, "lat", swap)
    w1, w2, a1, a2 = call(
        weights_body,
        "weights",
        [shape((c, TAPS * c), BF16)] * 4,
        [SMEM, VMEM, VMEM],
        (parity, own, other),
    )
    conv_flops = 2 * TAPS * c * c * height * lon
    columns = shape((height + 4, 3 * c, wide), BF16)
    middle = shape((height, c, wide), BF16)
    edge = shape((4, c, lon), BF16)
    fcol, ccol, hid, inn, up, down = call(
        functools.partial(first_body, step),
        "first",
        [columns, columns, middle, middle, edge, edge],
        [VMEM] * 6,
        (source, upstream, above, below, w1, a2),
        limit=20,
        flops=2 * conv_flops,
        nbytes=1 << 24,
    )
    hid_above, hid_below = edges(up, down)
    unit = 8 * bands
    rows = -(-SLABS * share // unit) * unit
    depth = rows // bands
    terms = call(
        functools.partial(terms_body, step, scale, shards),
        "terms",
        shape((2, bands // 2, shards, depth, LANES), F32),
        [VMEM] * 4,
        (fcol, ccol, hid, inn),
        scratch=[pltpu.VMEM((TAPS * c, c), F32)] * 2,
        limit=20,
        flops=2 * conv_flops,
        nbytes=1 << 24,
    )
    keep = lax.dynamic_index_in_dim(terms, parity[0], 0, keepdims=False)
    give = lax.dynamic_index_in_dim(terms, 1 - parity[0], 0, keepdims=False)
    pair = keep + lax.ppermute(give, "lat", swap)
    groups = [[i for i in range(bands) if i % 2 == p] for p in range(2)]
    got = lax.all_to_all(
        pair.astype(BF16), "lat", 0, 0, axis_index_groups=groups, tiled=True
    )
    column = jnp.sum(got.astype(F32), axis=0)
    got = lax.all_to_all(column.astype(BF16), "fsdp", 0, 0, tiled=True)
    chunk = jnp.sum(got.astype(F32), axis=0)
    chunks = lax.all_gather(chunk, "lat", axis=0)
    out, grad = call(
        functools.partial(second_body, step),
        "second",
        [shape((height, c, lon), BF16)] * 2,
        [VMEM] * 8,
        (source, upstream, hid, inn, hid_above, hid_below, w2, a1),
        scratch=[pltpu.VMEM(columns.shape, BF16)],
        limit=24,
        flops=2 * conv_flops,
        nbytes=1 << 24,
    )
    one, two = call(
        functools.partial(unpack_body, share),
        "unpack",
        [shape((TAPS, share, c), F32)] * 2,
        [VMEM],
        (chunks,),
    )
    return (
        jnp.swapaxes(out, 1, 2)[None],
        jnp.swapaxes(grad, 1, 2)[None],
        jnp.swapaxes(one, 1, 2).reshape(3, 3, c, share),
        jnp.swapaxes(two, 1, 2).reshape(3, 3, c, share),
    )


def solution(mesh):
    placed = (
        P("fsdp", "lat", None, None),
        P("fsdp", "lat", None, None),
        P(None, None, None, "fsdp"),
        P(None, None, None, "fsdp"),
    )
    return jax.shard_map(
        per_device,
        mesh=mesh,
        in_specs=placed,
        out_specs=placed,
        check_vma=False,
    )
```

```python
import functools

import jax
import jax.numpy as jnp
from jax import lax
from jax.experimental import pallas as pl
from jax.experimental.pallas import tpu as pltpu
from jax.sharding import PartitionSpec as P

BF16 = jnp.bfloat16
F32 = jnp.float32
VMEM = pl.BlockSpec(memory_space=pltpu.VMEM)
SMEM = pl.BlockSpec(memory_space=pltpu.SMEM)
ANY = pl.BlockSpec(memory_space=pltpu.HBM)
TAPS = 9
SLABS = TAPS + (TAPS + 1) // 2
HALF = SLABS // 2
LANES = 128
GROUP = 4
SPAN = 4


def shape(*dims, dtype=BF16):
    return jax.ShapeDtypeStruct(dims, dtype)


def call(body, name, outs, specs, args, scratch=(), limit=16, flops=0, nbytes=0):
    return pl.pallas_call(
        body,
        name=name,
        out_shape=[o for o, _ in outs],
        in_specs=specs,
        out_specs=[s for _, s in outs],
        scratch_shapes=list(scratch),
        compiler_params=pltpu.CompilerParams(vmem_limit_bytes=limit << 20),
        cost_estimate=pl.CostEstimate(flops=flops, bytes_accessed=nbytes, transcendentals=0),
    )(*args)


def to_slab(tap_of, s):
    if s < TAPS:
        return tap_of(s)[:, :LANES]
    first = 2 * (s - TAPS)
    second = min(first + 1, TAPS - 1)
    return jnp.concatenate([tap_of(first)[:, LANES:], tap_of(second)[:, LANES:]], axis=1)


def from_slabs(slab_of, tap):
    tails = slab_of(TAPS + tap // 2)
    half = LANES // 2
    tail = tails[:, half:] if tap % 2 else tails[:, :half]
    return jnp.concatenate([slab_of(tap), tail], axis=1)


def pack_body(parity, one, two, source, upstream, half, top, bottom, sem):
    height = source.shape[0]
    copies = []
    for base, rows in ((0, source), (2, upstream)):
        for k, (ref, at) in enumerate(((top, 0), (bottom, height - 2))):
            copies.append(
                pltpu.make_async_copy(
                    rows.at[pl.ds(at, 2)], ref.at[pl.ds(base, 2)], sem.at[base + k]
                )
            )
    for copy in copies:
        copy.start()
    for side in range(2):

        @pl.when(parity[0] == side)
        def _():
            for k, kernel in enumerate((one, two)):
                for i in range(HALF):
                    half[k * HALF + i] = to_slab(lambda tap: kernel[tap], side * HALF + i)

    for copy in copies:
        copy.wait()


def stack_body(place, half, *refs):
    out = refs[-1]
    for d, piece in enumerate((half,) + refs[:-1]):
        out[place[1] ^ d] = piece[...]


def load_weight(place, own, other, which, weight, adjoint):
    c = weight.shape[0]
    base = which * HALF
    mine = place[0] == 0
    slabs = {}

    def slab(s):
        if s not in slabs:
            side, i = divmod(s, HALF)
            first, second = (own, other) if side == 0 else (other, own)
            parts = [
                jnp.where(mine, first[f, base + i], second[f, base + i])
                for f in range(own.shape[0])
            ]
            slabs[s] = jnp.concatenate(parts, axis=0)
        return slabs[s]

    for tap in range(TAPS):
        value = from_slabs(slab, tap)
        if adjoint:
            weight[:, pl.ds((TAPS - 1 - tap) * c, c)] = value.T
        else:
            weight[:, pl.ds(tap * c, c)] = value


def store_row(columns, at, row):
    c, lon = row.shape
    fill = jnp.zeros((c, columns.shape[2] - lon), row.dtype)
    pieces = (
        jnp.concatenate([row[:, lon - 2 :], row[:, : lon - 2], fill], axis=1),
        jnp.concatenate([row, fill], axis=1),
        jnp.concatenate([row[:, 2:], row[:, :2], fill], axis=1),
    )
    for b, piece in enumerate(pieces):
        columns[at, b * c : (b + 1) * c] = piece


def taps_of(columns, at):
    return jnp.concatenate([columns[at], columns[at + 2], columns[at + 4]], axis=0)


def rows_of(columns, at, count=None):
    return jnp.concatenate([taps_of(columns, at + s) for s in range(count or GROUP)], axis=1)


def chunked(source, target, sem):
    return [
        pltpu.make_async_copy(
            source.at[pl.ds(at, GROUP)], target.at[pl.ds(at, GROUP)], sem.at[at // GROUP]
        )
        for at in range(0, source.shape[0], GROUP)
    ]


class Columns:
    def __init__(self, ref, rows, copies, base, lon):
        self.ref, self.rows, self.copies = ref, rows, copies
        self.base, self.lon = base, lon
        self.done = 0

    def fill(self, upto):
        while self.done < min(upto, self.rows.shape[0]):
            if self.done % GROUP == 0:
                self.copies[self.done // GROUP].wait()
            store_row(self.ref, self.done + self.base, self.rows[self.done][:, : self.lon])
            self.done += 1


def place_terms(out, base, depth, total, shards, scale, flip):
    c = total.shape[1]
    share = c // shards
    values = {}

    def tap_of(tap):
        if tap not in values:
            if flip:
                values[tap] = total[tap * c : (tap + 1) * c].T * scale
            else:
                values[tap] = total[(TAPS - 1 - tap) * c : (TAPS - tap) * c] * scale
        return values[tap]

    for s in range(SLABS):
        value = to_slab(tap_of, s).astype(BF16)
        for f in range(shards):
            start = s * share
            while start < (s + 1) * share:
                chunk, inside = divmod(start, depth)
                stop = min((s + 1) * share, (chunk + 1) * depth)
                src = f * share + start - s * share
                lo = base + inside
                out[chunk, f, lo : lo + stop - start] = value[src : src + stop - start]
                start = stop


def sum_terms(total, columns, field):
    total[...] = jnp.zeros_like(total)

    def work(t, carry):
        at = t * SPAN
        rhs = jnp.concatenate([field[at + s] for s in range(SPAN)], axis=1)
        total[...] += lax.dot_general(
            rows_of(columns, at, SPAN),
            rhs,
            (((1,), (1,)), ((), ())),
            preferred_element_type=F32,
        )
        return carry

    lax.fori_loop(0, field.shape[0] // SPAN, work, 0)


def stage_body(
    scale, shards, place, source, upstream, above, below, own, other,
    hid, inn, top, bottom, terms,
    src, ups, fcol, ccol, w1, a2, hidden, inner, one, two, sem, edge_sem,
):
    height, _, lon = source.shape
    wide = fcol.shape[2]
    loads = [chunked(source, src, sem.at[0]), chunked(upstream, ups, sem.at[1])]
    for pair in zip(*loads):
        for copy in pair:
            copy.start()
    load_weight(place, own, other, 0, w1, False)
    load_weight(place, own, other, 1, a2, True)
    for columns, base in ((fcol, 0), (ccol, 2)):
        for r in range(2):
            store_row(columns, r, above[base + r])
            store_row(columns, height + 2 + r, below[base + r])
    forward = Columns(fcol, src, loads[0], 2, lon)
    reverse = Columns(ccol, ups, loads[1], 2, lon)
    forward.fill(GROUP + 2)
    saves = [chunked(hidden, hid, sem.at[2]), chunked(inner, inn, sem.at[3])]
    edges = []
    for k, rows in enumerate((hidden, inner)):
        for j, (ref, at) in enumerate(((top, 0), (bottom, height - 2))):
            edges.append(
                pltpu.make_async_copy(
                    rows.at[pl.ds(at, 2)], ref.at[pl.ds(2 * k, 2)], edge_sem.at[2 * k + j]
                )
            )
    for at in range(0, height, GROUP):
        reverse.fill(at + GROUP + 2)
        pre = jnp.dot(w1[...], rows_of(fcol, at), preferred_element_type=F32)
        forward.fill(at + 2 * GROUP + 2)
        back = jnp.dot(a2[...], rows_of(ccol, at), preferred_element_type=F32)
        cdf = 0.5 * (1.0 + lax.erf(pre * 0.7071067811865476))
        value = (pre * cdf).astype(BF16)
        rate = cdf + pre * jnp.exp(-0.5 * pre * pre) * 0.3989422804014327
        grad = (back * rate).astype(BF16)
        for s in range(GROUP):
            hidden[at + s] = value[:, s * wide : (s + 1) * wide]
            inner[at + s] = grad[:, s * wide : (s + 1) * wide]
        for save in saves:
            save[at // GROUP].start()
    for copy in edges:
        copy.start()
    sum_terms(one, fcol, inner)
    sum_terms(two, ccol, hidden)
    depth = terms.shape[2] // 2
    place_terms(terms, 0, depth, one, shards, scale, True)
    place_terms(terms, depth, depth, two, shards, scale, False)
    for copy in saves[0] + saves[1] + edges:
        copy.wait()


def interior_body(
    place, source, upstream, hid, inn, own, other,
    out, grad, w2, a1,
    src, ups, mid, cot, hcol, icol, left, right, sem,
):
    height, _, lon = source.shape
    wide = hcol.shape[2]
    work = []
    for k, args in enumerate(
        ((hid, mid, hcol, source, src, w2, left, out), (inn, cot, icol, upstream, ups, a1, right, grad))
    ):
        middle, held, columns, residual, base, weight, result, target = args
        loads = [chunked(middle, held, sem.at[3 * k]), chunked(residual, base, sem.at[3 * k + 1])]
        for pair in zip(*loads):
            for copy in pair:
                copy.start()
        rows = Columns(columns, held, loads[0], 0, lon)
        work.append((rows, loads[1], columns, base, weight, result, target, sem.at[3 * k + 2]))
    load_weight(place, own, other, 1, w2, False)
    load_weight(place, own, other, 0, a1, True)
    saves = []
    for rows, waits, columns, base, weight, result, target, done in work:
        rows.fill(GROUP + 4)
        waits[0].wait()
        for at in range(0, height - 4, GROUP):
            waits[at // GROUP + 1].wait()
            rows.fill(at + 2 * GROUP + 4)
            value = jnp.dot(weight[...], rows_of(columns, at), preferred_element_type=F32)
            for s in range(GROUP):
                part = value[:, s * wide : s * wide + lon]
                row = at + 2 + s
                result[row] = (base[row].astype(F32) + part).astype(BF16)
            span = pl.ds(at + 2, GROUP)
            save = pltpu.make_async_copy(result.at[span], target.at[span], done.at[at // GROUP])
            save.start()
            saves.append(save)
    for save in saves:
        save.wait()


def edge_body(
    source, upstream, hid, inn, above, below, w2, a1, out_in, grad_in,
    out, grad,
    res, mid, columns, result, sem,
):
    del out_in, grad_in
    height, _, lon = source.shape
    wide = columns.shape[3]
    ends = (0, height - 4), (0, height - 2)
    loads, saves = [], []
    for k, (residual, middle, target) in enumerate(((source, hid, out), (upstream, inn, grad))):
        for j in range(2):
            loads.append(
                pltpu.make_async_copy(
                    middle.at[pl.ds(ends[0][j], 4)], mid.at[2 * k + j], sem.at[0, 2 * k + j]
                )
            )
            loads.append(
                pltpu.make_async_copy(
                    residual.at[pl.ds(ends[1][j], 2)], res.at[2 * k + j], sem.at[1, 2 * k + j]
                )
            )
            saves.append(
                pltpu.make_async_copy(
                    result.at[2 * k + j], target.at[pl.ds(ends[1][j], 2)], sem.at[2, 2 * k + j]
                )
            )
    for copy in loads:
        copy.start()
    for k in range(2):
        for r in range(2):
            store_row(columns.at[2 * k], r, above[2 * k + r][:, :lon])
            store_row(columns.at[2 * k + 1], 4 + r, below[2 * k + r][:, :lon])
    for k, weight in enumerate((w2, a1)):
        for j in range(2):
            for copy in loads[4 * k + 2 * j : 4 * k + 2 * j + 2]:
                copy.wait()
            for r in range(4):
                store_row(columns.at[2 * k + j], r + 2 - 2 * j, mid[2 * k + j, r][:, :lon])
        rhs = jnp.concatenate(
            [taps_of(columns.at[2 * k + j], r) for j in range(2) for r in range(2)], axis=1
        )
        value = jnp.dot(weight[...], rhs, preferred_element_type=F32)
        for j in range(2):
            for r in range(2):
                lo = (2 * j + r) * wide
                part = value[:, lo : lo + lon]
                base = res[2 * k + j, r].astype(F32)
                result[2 * k + j, r] = (base + part).astype(BF16)
            saves[2 * k + j].start()
    for copy in saves:
        copy.wait()


def column_body(place, got, mine, *gives):
    def total(f):
        value = got[0, f].astype(F32)
        for i in range(1, got.shape[0]):
            value += got[i, f].astype(F32)
        return value

    mine[...] = total(place[1])
    for d, give in enumerate(gives):
        give[...] = total(place[1] ^ (d + 1)).astype(BF16)


def chunk_body(mine, *refs):
    total = mine[...]
    for piece in refs[:-1]:
        total += piece[...].astype(F32)
    refs[-1][...] = total


def unpack_body(share, depth, chunks, one, two):
    for k, result in enumerate((one, two)):

        def slab(s):
            parts = []
            start = s * share
            while start < (s + 1) * share:
                chunk, inside = divmod(start, depth)
                stop = min((s + 1) * share, (chunk + 1) * depth)
                lo = k * depth + inside
                parts.append(chunks[chunk, lo : lo + stop - start])
                start = stop
            return parts[0] if len(parts) == 1 else jnp.concatenate(parts, axis=0)

        for tap in range(TAPS):
            result[tap] = from_slabs(slab, tap)


def per_device(fields, cotangent, kernel_one, kernel_two):
    _, height, lon, c = fields.shape
    share = kernel_one.shape[3]
    shards = lax.axis_size("fsdp")
    bands = lax.axis_size("lat")
    wide = -(-lon // LANES) * LANES
    scale = 1.0 / (shards * fields.shape[0] * bands * height * lon) ** 0.5
    source = jnp.swapaxes(fields[0], 1, 2)
    upstream = jnp.swapaxes(cotangent[0], 1, 2)
    small = [
        jnp.swapaxes(k.reshape(TAPS, c, share), 1, 2) for k in (kernel_one, kernel_two)
    ]
    place = jnp.stack([lax.axis_index("lat") % 2, lax.axis_index("fsdp")]).astype(jnp.int32)
    forward = [(i, i + 1) for i in range(bands - 1)]
    backward = [(i + 1, i) for i in range(bands - 1)]
    swap = [(i, i ^ 1) for i in range(bands)]

    def edges(top, bottom):
        return lax.ppermute(bottom, "lat", forward), lax.ppermute(top, "lat", backward)

    def partner(value, d):
        return lax.ppermute(value, "fsdp", [(i, i ^ d) for i in range(shards)])

    conv_flops = 2 * TAPS * c * c * height * lon
    groups = height // GROUP
    depth = -(-SLABS * share // (8 * bands)) * 8
    others = range(1, shards)
    half, top, bottom = call(
        pack_body,
        "pack",
        [
            (shape(2 * HALF, share, LANES), VMEM),
            (shape(4, c, lon), ANY),
            (shape(4, c, lon), ANY),
        ],
        [SMEM, VMEM, VMEM, ANY, ANY],
        (place, *small, source, upstream),
        scratch=[pltpu.SemaphoreType.DMA((4,))],
    )
    pieces = [partner(half, d) for d in others]
    above, below = edges(top, bottom)
    (own,) = call(
        stack_body,
        "stack",
        [(shape(shards, 2 * HALF, share, LANES), VMEM)],
        [SMEM] + [VMEM] * shards,
        (place, half, *pieces),
    )
    other = lax.ppermute(own, "lat", swap)

    middle = shape(height, c, wide)
    edge = shape(4, c, wide)
    plain = pltpu.VMEM((height, c, lon), BF16)
    lined = pltpu.VMEM((height, c, wide), BF16)
    columns = pltpu.VMEM((height + 4, 3 * c, wide), BF16)
    matrix = pltpu.VMEM((c, TAPS * c), BF16)
    total = pltpu.VMEM((TAPS * c, c), F32)
    hid, inn, top, bottom, terms = call(
        functools.partial(stage_body, scale, shards),
        "stage",
        [
            (middle, ANY),
            (middle, ANY),
            (edge, ANY),
            (edge, ANY),
            (shape(bands, shards, 2 * depth, LANES), VMEM),
        ],
        [SMEM, ANY, ANY, VMEM, VMEM, VMEM, VMEM],
        (place, source, upstream, above, below, own, other),
        scratch=[plain, plain, columns, columns, matrix, matrix, lined, lined, total, total]
        + [pltpu.SemaphoreType.DMA((4, groups)), pltpu.SemaphoreType.DMA((4,))],
        limit=52,
        flops=4 * conv_flops,
        nbytes=1 << 24,
    )
    above, below = edges(top, bottom)
    got = lax.all_to_all(terms, "lat", 0, 0, tiled=True)
    columns = pltpu.VMEM((height, 3 * c, wide), BF16)
    outs = (shape(height, c, lon), ANY)
    weight = (shape(c, TAPS * c), VMEM)
    out, grad, w2, a1 = call(
        interior_body,
        "interior",
        [outs, outs, weight, weight],
        [SMEM, ANY, ANY, ANY, ANY, VMEM, VMEM],
        (place, source, upstream, hid, inn, own, other),
        scratch=[plain, plain, lined, lined, columns, columns, plain, plain]
        + [pltpu.SemaphoreType.DMA((6, groups))],
        limit=50,
        flops=2 * conv_flops,
        nbytes=1 << 24,
    )
    mine, *gives = call(
        column_body,
        "column",
        [(shape(2 * depth, LANES, dtype=F32), VMEM)]
        + [(shape(2 * depth, LANES), VMEM) for _ in others],
        [SMEM, VMEM],
        (place, got),
    )
    gains = [partner(give, d) for d, give in zip(others, gives)]
    out, grad = pl.pallas_call(
        edge_body,
        name="edge",
        out_shape=[outs[0], outs[0]],
        in_specs=[ANY] * 4 + [VMEM] * 4 + [ANY] * 2,
        out_specs=[ANY, ANY],
        input_output_aliases={8: 0, 9: 1},
        scratch_shapes=[
            pltpu.VMEM((4, 2, c, lon), BF16),
            pltpu.VMEM((4, 4, c, wide), BF16),
            pltpu.VMEM((4, 6, 3 * c, wide), BF16),
            pltpu.VMEM((4, 2, c, lon), BF16),
            pltpu.SemaphoreType.DMA((3, 4)),
        ],
        compiler_params=pltpu.CompilerParams(vmem_limit_bytes=32 << 20),
        cost_estimate=pl.CostEstimate(
            flops=conv_flops // 2, bytes_accessed=1 << 22, transcendentals=0
        ),
    )(source, upstream, hid, inn, above, below, w2, a1, out, grad)
    (chunk,) = call(
        chunk_body,
        "chunk",
        [(shape(2 * depth, LANES, dtype=F32), VMEM)],
        [VMEM] * shards,
        (mine, *gains),
    )
    chunks = lax.all_gather(chunk, "lat", axis=0)
    one, two = call(
        functools.partial(unpack_body, share, depth),
        "unpack",
        [(shape(TAPS, share, c, dtype=F32), VMEM)] * 2,
        [VMEM],
        (chunks,),
    )
    return (
        jnp.swapaxes(out, 1, 2)[None],
        jnp.swapaxes(grad, 1, 2)[None],
        jnp.swapaxes(one, 1, 2).reshape(3, 3, c, share),
        jnp.swapaxes(two, 1, 2).reshape(3, 3, c, share),
    )


def solution(mesh):
    placed = (
        P("fsdp", "lat", None, None),
        P("fsdp", "lat", None, None),
        P(None, None, None, "fsdp"),
        P(None, None, None, "fsdp"),
    )
    return jax.shard_map(
        per_device,
        mesh=mesh,
        in_specs=placed,
        out_specs=placed,
        check_vma=False,
    )
```

```python
import functools

import jax
import jax.numpy as jnp
from jax import lax
from jax.experimental import pallas as pl
from jax.experimental.pallas import tpu as pltpu
from jax.sharding import PartitionSpec as P

BF16 = jnp.bfloat16
F32 = jnp.float32
VMEM = pl.BlockSpec(memory_space=pltpu.VMEM)
SMEM = pl.BlockSpec(memory_space=pltpu.SMEM)
ANY = pl.BlockSpec(memory_space=pltpu.HBM)
TAPS = 9
SLABS = TAPS + (TAPS + 1) // 2
HALF = SLABS // 2
LANES = 128
GROUP = 4
SPAN = 4


def shape(*dims, dtype=BF16):
    return jax.ShapeDtypeStruct(dims, dtype)


def call(body, name, outs, specs, args, scratch=(), limit=16, flops=0, nbytes=0):
    return pl.pallas_call(
        body,
        name=name,
        out_shape=[o for o, _ in outs],
        in_specs=specs,
        out_specs=[s for _, s in outs],
        scratch_shapes=list(scratch),
        compiler_params=pltpu.CompilerParams(vmem_limit_bytes=limit << 20),
        cost_estimate=pl.CostEstimate(flops=flops, bytes_accessed=nbytes, transcendentals=0),
    )(*args)


def to_slab(tap_of, s):
    if s < TAPS:
        return tap_of(s)[:, :LANES]
    first = 2 * (s - TAPS)
    second = min(first + 1, TAPS - 1)
    return jnp.concatenate([tap_of(first)[:, LANES:], tap_of(second)[:, LANES:]], axis=1)


def from_slabs(slab_of, tap):
    tails = slab_of(TAPS + tap // 2)
    half = LANES // 2
    tail = tails[:, half:] if tap % 2 else tails[:, :half]
    return jnp.concatenate([slab_of(tap), tail], axis=1)


def pack_body(
    parity, first, second, source, upstream, half, top, bottom, one, two, sem
):
    height = source.shape[0]
    copies = [
        pltpu.make_async_copy(first, one, sem.at[4]),
        pltpu.make_async_copy(second, two, sem.at[5]),
    ]
    for base, rows in ((0, source), (2, upstream)):
        for k, (ref, at) in enumerate(((top, 0), (bottom, height - 2))):
            copies.append(
                pltpu.make_async_copy(
                    rows.at[pl.ds(at, 2)], ref.at[pl.ds(base, 2)], sem.at[base + k]
                )
            )
    for copy in copies:
        copy.start()
    copies[0].wait()
    copies[1].wait()
    for side in range(2):

        @pl.when(parity[0] == side)
        def _():
            for k, kernel in enumerate((one, two)):
                for i in range(HALF):
                    half[k * HALF + i] = to_slab(lambda tap: kernel[tap], side * HALF + i)

    for copy in copies[2:]:
        copy.wait()


def stack_body(place, half, *refs):
    *pieces, _, _, out = refs
    for d, piece in enumerate([half] + pieces):
        out[place[1] ^ d] = piece[...]


def load_weight(place, own, other, which, weight, adjoint):
    c = weight.shape[0]
    base = which * HALF
    mine = place[0] == 0
    slabs = {}

    def slab(s):
        if s not in slabs:
            side, i = divmod(s, HALF)
            first, second = (own, other) if side == 0 else (other, own)
            parts = [
                jnp.where(mine, first[f, base + i], second[f, base + i])
                for f in range(own.shape[0])
            ]
            slabs[s] = jnp.concatenate(parts, axis=0)
        return slabs[s]

    for tap in range(TAPS):
        value = from_slabs(slab, tap)
        if adjoint:
            weight[:, pl.ds((TAPS - 1 - tap) * c, c)] = value.T
        else:
            weight[:, pl.ds(tap * c, c)] = value


def store_row(columns, at, row):
    c, lon = row.shape
    fill = jnp.zeros((c, columns.shape[2] - lon), row.dtype)
    pieces = (
        jnp.concatenate([row[:, lon - 2 :], row[:, : lon - 2], fill], axis=1),
        jnp.concatenate([row, fill], axis=1),
        jnp.concatenate([row[:, 2:], row[:, :2], fill], axis=1),
    )
    for b, piece in enumerate(pieces):
        columns[at, b * c : (b + 1) * c] = piece


def taps_of(columns, at):
    return jnp.concatenate([columns[at], columns[at + 2], columns[at + 4]], axis=0)


def rows_of(columns, at, count=None):
    return jnp.concatenate([taps_of(columns, at + s) for s in range(count or GROUP)], axis=1)


def chunked(source, target, sem):
    return [
        pltpu.make_async_copy(
            source.at[pl.ds(at, GROUP)], target.at[pl.ds(at, GROUP)], sem.at[at // GROUP]
        )
        for at in range(0, source.shape[0], GROUP)
    ]


class Columns:
    def __init__(self, ref, rows, copies, base, lon):
        self.ref, self.rows, self.copies = ref, rows, copies
        self.base, self.lon = base, lon
        self.done = 0

    def fill(self, upto):
        while self.done < min(upto, self.rows.shape[0]):
            if self.done % GROUP == 0:
                self.copies[self.done // GROUP].wait()
            store_row(self.ref, self.done + self.base, self.rows[self.done][:, : self.lon])
            self.done += 1


def place_terms(out, base, depth, total, shards, scale, flip):
    c = total.shape[1]
    share = c // shards
    values = {}

    def tap_of(tap):
        if tap not in values:
            if flip:
                values[tap] = total[tap * c : (tap + 1) * c].T * scale
            else:
                values[tap] = total[(TAPS - 1 - tap) * c : (TAPS - tap) * c] * scale
        return values[tap]

    for s in range(SLABS):
        value = to_slab(tap_of, s).astype(BF16)
        for f in range(shards):
            start = s * share
            while start < (s + 1) * share:
                chunk, inside = divmod(start, depth)
                stop = min((s + 1) * share, (chunk + 1) * depth)
                src = f * share + start - s * share
                lo = base + inside
                out[chunk, f, lo : lo + stop - start] = value[src : src + stop - start]
                start = stop


def sum_terms(total, columns, field):
    total[...] = jnp.zeros_like(total)

    def work(t, carry):
        at = t * SPAN
        rhs = jnp.concatenate([field[at + s] for s in range(SPAN)], axis=1)
        total[...] += lax.dot_general(
            rows_of(columns, at, SPAN),
            rhs,
            (((1,), (1,)), ((), ())),
            preferred_element_type=F32,
        )
        return carry

    lax.fori_loop(0, field.shape[0] // SPAN, work, 0)


def stage_body(
    scale, shards, place, source, upstream, above_in, below_in, own_in, other_in,
    hid, inn, top, bottom, terms,
    src, ups, fcol, ccol, w1, a2, hidden, inner, one, two, above, below, own, other,
    sem, edge_sem,
):
    height, _, lon = source.shape
    wide = fcol.shape[2]
    firsts = [
        pltpu.make_async_copy(a, b, edge_sem.at[4 + k])
        for k, (a, b) in enumerate(
            ((own_in, own), (other_in, other), (above_in, above), (below_in, below))
        )
    ]
    for copy in firsts:
        copy.start()
    loads = [chunked(source, src, sem.at[0]), chunked(upstream, ups, sem.at[1])]
    for pair in zip(*loads):
        for copy in pair:
            copy.start()
    firsts[0].wait()
    firsts[1].wait()
    load_weight(place, own, other, 0, w1, False)
    load_weight(place, own, other, 1, a2, True)
    firsts[2].wait()
    firsts[3].wait()
    for columns, base in ((fcol, 0), (ccol, 2)):
        for r in range(2):
            store_row(columns, r, above[base + r])
            store_row(columns, height + 2 + r, below[base + r])
    forward = Columns(fcol, src, loads[0], 2, lon)
    reverse = Columns(ccol, ups, loads[1], 2, lon)
    forward.fill(GROUP + 2)
    saves = [chunked(hidden, hid, sem.at[2]), chunked(inner, inn, sem.at[3])]
    edges = []
    for k, rows in enumerate((hidden, inner)):
        for j, (ref, at) in enumerate(((top, 0), (bottom, height - 2))):
            edges.append(
                pltpu.make_async_copy(
                    rows.at[pl.ds(at, 2)], ref.at[pl.ds(2 * k, 2)], edge_sem.at[2 * k + j]
                )
            )
    for at in range(0, height, GROUP):
        reverse.fill(at + GROUP + 2)
        pre = jnp.dot(w1[...], rows_of(fcol, at), preferred_element_type=F32)
        forward.fill(at + 2 * GROUP + 2)
        back = jnp.dot(a2[...], rows_of(ccol, at), preferred_element_type=F32)
        cdf = 0.5 * (1.0 + lax.erf(pre * 0.7071067811865476))
        value = (pre * cdf).astype(BF16)
        rate = cdf + pre * jnp.exp(-0.5 * pre * pre) * 0.3989422804014327
        grad = (back * rate).astype(BF16)
        for s in range(GROUP):
            hidden[at + s] = value[:, s * wide : (s + 1) * wide]
            inner[at + s] = grad[:, s * wide : (s + 1) * wide]
        for save in saves:
            save[at // GROUP].start()
    for copy in edges:
        copy.start()
    sum_terms(one, fcol, inner)
    sum_terms(two, ccol, hidden)
    depth = terms.shape[2] // 2
    place_terms(terms, 0, depth, one, shards, scale, True)
    place_terms(terms, depth, depth, two, shards, scale, False)
    for copy in saves[0] + saves[1] + edges:
        copy.wait()


def interior_body(
    place, source, upstream, hid, inn, own_in, other_in,
    out, grad, w2_out, a1_out,
    src, ups, mid, cot, hcol, icol, left, right, w2, a1, own, other, sem, weight_sem,
):
    height, _, lon = source.shape
    wide = hcol.shape[2]
    firsts = [
        pltpu.make_async_copy(a, b, weight_sem.at[k])
        for k, (a, b) in enumerate(((own_in, own), (other_in, other)))
    ]
    for copy in firsts:
        copy.start()
    work = []
    for k, args in enumerate(
        ((hid, mid, hcol, source, src, w2, left, out), (inn, cot, icol, upstream, ups, a1, right, grad))
    ):
        middle, held, columns, residual, base, weight, result, target = args
        loads = [chunked(middle, held, sem.at[3 * k]), chunked(residual, base, sem.at[3 * k + 1])]
        for pair in zip(*loads):
            for copy in pair:
                copy.start()
        rows = Columns(columns, held, loads[0], 0, lon)
        work.append((rows, loads[1], columns, base, weight, result, target, sem.at[3 * k + 2]))
    work[0][0].fill(2 * GROUP)
    for copy in firsts:
        copy.wait()
    load_weight(place, own, other, 1, w2, False)
    load_weight(place, own, other, 0, a1, True)
    saves = [
        pltpu.make_async_copy(a, b, weight_sem.at[2 + k])
        for k, (a, b) in enumerate(((w2, w2_out), (a1, a1_out)))
    ]
    for save in saves:
        save.start()
    for rows, waits, columns, base, weight, result, target, done in work:
        rows.fill(GROUP + 4)
        waits[0].wait()
        for at in range(0, height - 4, GROUP):
            waits[at // GROUP + 1].wait()
            rows.fill(at + 2 * GROUP + 4)
            value = jnp.dot(weight[...], rows_of(columns, at), preferred_element_type=F32)
            for s in range(GROUP):
                part = value[:, s * wide : s * wide + lon]
                row = at + 2 + s
                result[row] = (base[row].astype(F32) + part).astype(BF16)
            span = pl.ds(at + 2, GROUP)
            save = pltpu.make_async_copy(result.at[span], target.at[span], done.at[at // GROUP])
            save.start()
            saves.append(save)
    for save in saves:
        save.wait()


def edge_body(
    source, upstream, hid, inn, above_in, below_in, w2_in, a1_in, out_in, grad_in,
    out, grad,
    res, mid, columns, result, above, below, w2, a1, sem,
):
    del out_in, grad_in
    firsts = [
        pltpu.make_async_copy(a, b, sem.at[3, k])
        for k, (a, b) in enumerate(
            ((above_in, above), (below_in, below), (w2_in, w2), (a1_in, a1))
        )
    ]
    for copy in firsts:
        copy.start()
    height, _, lon = source.shape
    wide = columns.shape[3]
    ends = (0, height - 4), (0, height - 2)
    loads, saves = [], []
    for k, (residual, middle, target) in enumerate(((source, hid, out), (upstream, inn, grad))):
        for j in range(2):
            loads.append(
                pltpu.make_async_copy(
                    middle.at[pl.ds(ends[0][j], 4)], mid.at[2 * k + j], sem.at[0, 2 * k + j]
                )
            )
            loads.append(
                pltpu.make_async_copy(
                    residual.at[pl.ds(ends[1][j], 2)], res.at[2 * k + j], sem.at[1, 2 * k + j]
                )
            )
            saves.append(
                pltpu.make_async_copy(
                    result.at[2 * k + j], target.at[pl.ds(ends[1][j], 2)], sem.at[2, 2 * k + j]
                )
            )
    for copy in loads:
        copy.start()
    firsts[0].wait()
    firsts[1].wait()
    for k in range(2):
        for r in range(2):
            store_row(columns.at[2 * k], r, above[2 * k + r][:, :lon])
            store_row(columns.at[2 * k + 1], 4 + r, below[2 * k + r][:, :lon])
    for k, weight in enumerate((w2, a1)):
        for j in range(2):
            for copy in loads[4 * k + 2 * j : 4 * k + 2 * j + 2]:
                copy.wait()
            for r in range(4):
                store_row(columns.at[2 * k + j], r + 2 - 2 * j, mid[2 * k + j, r][:, :lon])
        rhs = jnp.concatenate(
            [taps_of(columns.at[2 * k + j], r) for j in range(2) for r in range(2)], axis=1
        )
        firsts[2 + k].wait()
        value = jnp.dot(weight[...], rhs, preferred_element_type=F32)
        for j in range(2):
            for r in range(2):
                lo = (2 * j + r) * wide
                part = value[:, lo : lo + lon]
                base = res[2 * k + j, r].astype(F32)
                result[2 * k + j, r] = (base + part).astype(BF16)
            saves[2 * k + j].start()
    for copy in saves:
        copy.wait()


def column_body(place, got, mine, *gives):
    def total(f):
        value = got[0, f].astype(F32)
        for i in range(1, got.shape[0]):
            value += got[i, f].astype(F32)
        return value

    mine[...] = total(place[1])
    for d, give in enumerate(gives):
        give[...] = total(place[1] ^ (d + 1)).astype(BF16)


def chunk_body(mine, *refs):
    total = mine[...]
    for piece in refs[:-1]:
        total += piece[...].astype(F32)
    refs[-1][...] = total


def unpack_body(share, depth, chunks, one, two):
    for k, result in enumerate((one, two)):

        def slab(s):
            parts = []
            start = s * share
            while start < (s + 1) * share:
                chunk, inside = divmod(start, depth)
                stop = min((s + 1) * share, (chunk + 1) * depth)
                lo = k * depth + inside
                parts.append(chunks[chunk, lo : lo + stop - start])
                start = stop
            return parts[0] if len(parts) == 1 else jnp.concatenate(parts, axis=0)

        for tap in range(TAPS):
            result[tap] = from_slabs(slab, tap)


def per_device(fields, cotangent, kernel_one, kernel_two):
    _, height, lon, c = fields.shape
    share = kernel_one.shape[3]
    shards = lax.axis_size("fsdp")
    bands = lax.axis_size("lat")
    wide = -(-lon // LANES) * LANES
    scale = 1.0 / (shards * fields.shape[0] * bands * height * lon) ** 0.5
    source = jnp.swapaxes(fields[0], 1, 2)
    upstream = jnp.swapaxes(cotangent[0], 1, 2)
    small = [
        jnp.swapaxes(k.reshape(TAPS, c, share), 1, 2) for k in (kernel_one, kernel_two)
    ]
    place = jnp.stack([lax.axis_index("lat") % 2, lax.axis_index("fsdp")]).astype(jnp.int32)
    forward = [(i, i + 1) for i in range(bands - 1)]
    backward = [(i + 1, i) for i in range(bands - 1)]
    swap = [(i, i ^ 1) for i in range(bands)]

    def edges(top, bottom):
        return lax.ppermute(bottom, "lat", forward), lax.ppermute(top, "lat", backward)

    def partner(value, d):
        return lax.ppermute(value, "fsdp", [(i, i ^ d) for i in range(shards)])

    conv_flops = 2 * TAPS * c * c * height * lon
    groups = height // GROUP
    depth = -(-SLABS * share // (8 * bands)) * 8
    others = range(1, shards)
    half, top, bottom = call(
        pack_body,
        "pack",
        [
            (shape(2 * HALF, share, LANES), VMEM),
            (shape(4, c, lon), VMEM),
            (shape(4, c, lon), VMEM),
        ],
        [SMEM, ANY, ANY, ANY, ANY],
        (place, *small, source, upstream),
        scratch=[pltpu.VMEM((TAPS, share, c), BF16)] * 2 + [pltpu.SemaphoreType.DMA((6,))],
        limit=60,
    )
    pieces = [partner(half, d) for d in others]
    above, below = edges(top, bottom)
    (own,) = call(
        stack_body,
        "stack",
        [(shape(shards, 2 * HALF, share, LANES), VMEM)],
        [SMEM] + [VMEM] * shards + [ANY, ANY],
        (place, half, *pieces, above, below),
    )
    other = lax.ppermute(own, "lat", swap)

    middle = shape(height, c, wide)
    edge = shape(4, c, wide)
    plain = pltpu.VMEM((height, c, lon), BF16)
    lined = pltpu.VMEM((height, c, wide), BF16)
    columns = pltpu.VMEM((height + 4, 3 * c, wide), BF16)
    matrix = pltpu.VMEM((c, TAPS * c), BF16)
    total = pltpu.VMEM((TAPS * c, c), F32)
    halo = pltpu.VMEM((4, c, lon), BF16)
    gathered = pltpu.VMEM(own.shape, BF16)
    hid, inn, top, bottom, terms = call(
        functools.partial(stage_body, scale, shards),
        "stage",
        [
            (middle, ANY),
            (middle, ANY),
            (edge, ANY),
            (edge, ANY),
            (shape(bands, shards, 2 * depth, LANES), VMEM),
        ],
        [SMEM] + [ANY] * 6,
        (place, source, upstream, above, below, own, other),
        scratch=[plain, plain, columns, columns, matrix, matrix, lined, lined, total, total]
        + [halo, halo, gathered, gathered]
        + [pltpu.SemaphoreType.DMA((4, groups)), pltpu.SemaphoreType.DMA((8,))],
        limit=60,
        flops=4 * conv_flops,
        nbytes=1 << 24,
    )
    above, below = edges(top, bottom)
    got = lax.all_to_all(terms, "lat", 0, 0, tiled=True)
    columns = pltpu.VMEM((height, 3 * c, wide), BF16)
    outs = (shape(height, c, lon), ANY)
    weight = (shape(c, TAPS * c), ANY)
    out, grad, w2, a1 = call(
        interior_body,
        "interior",
        [outs, outs, weight, weight],
        [SMEM] + [ANY] * 6,
        (place, source, upstream, hid, inn, own, other),
        scratch=[plain, plain, lined, lined, columns, columns, plain, plain]
        + [matrix, matrix, gathered, gathered]
        + [pltpu.SemaphoreType.DMA((6, groups)), pltpu.SemaphoreType.DMA((4,))],
        limit=60,
        flops=2 * conv_flops,
        nbytes=1 << 24,
    )
    mine, *gives = call(
        column_body,
        "column",
        [(shape(2 * depth, LANES, dtype=F32), VMEM)]
        + [(shape(2 * depth, LANES), VMEM) for _ in others],
        [SMEM, VMEM],
        (place, got),
    )
    gains = [partner(give, d) for d, give in zip(others, gives)]
    out, grad = pl.pallas_call(
        edge_body,
        name="edge",
        out_shape=[outs[0], outs[0]],
        in_specs=[ANY] * 10,
        out_specs=[ANY, ANY],
        input_output_aliases={8: 0, 9: 1},
        scratch_shapes=[
            pltpu.VMEM((4, 2, c, lon), BF16),
            pltpu.VMEM((4, 4, c, wide), BF16),
            pltpu.VMEM((4, 6, 3 * c, wide), BF16),
            pltpu.VMEM((4, 2, c, lon), BF16),
            pltpu.VMEM(edge.shape, BF16),
            pltpu.VMEM(edge.shape, BF16),
            matrix,
            matrix,
            pltpu.SemaphoreType.DMA((4, 4)),
        ],
        compiler_params=pltpu.CompilerParams(vmem_limit_bytes=60 << 20),
        cost_estimate=pl.CostEstimate(
            flops=conv_flops // 2, bytes_accessed=1 << 22, transcendentals=0
        ),
    )(source, upstream, hid, inn, above, below, w2, a1, out, grad)
    (chunk,) = call(
        chunk_body,
        "chunk",
        [(shape(2 * depth, LANES, dtype=F32), VMEM)],
        [VMEM] * shards,
        (mine, *gains),
    )
    chunks = lax.all_gather(chunk, "lat", axis=0)
    one, two = call(
        functools.partial(unpack_body, share, depth),
        "unpack",
        [(shape(TAPS, share, c, dtype=F32), VMEM)] * 2,
        [VMEM],
        (chunks,),
    )
    return (
        jnp.swapaxes(out, 1, 2)[None],
        jnp.swapaxes(grad, 1, 2)[None],
        jnp.swapaxes(one, 1, 2).reshape(3, 3, c, share),
        jnp.swapaxes(two, 1, 2).reshape(3, 3, c, share),
    )


def solution(mesh):
    placed = (
        P("fsdp", "lat", None, None),
        P("fsdp", "lat", None, None),
        P(None, None, None, "fsdp"),
        P(None, None, None, "fsdp"),
    )
    return jax.shard_map(
        per_device,
        mesh=mesh,
        in_specs=placed,
        out_specs=placed,
        check_vma=False,
    )
```

```python
import functools

import jax
import jax.numpy as jnp
from jax import lax
from jax.experimental import pallas as pl
from jax.experimental.pallas import tpu as pltpu
from jax.sharding import PartitionSpec as P

BF16 = jnp.bfloat16
F32 = jnp.float32
VMEM = pl.BlockSpec(memory_space=pltpu.VMEM)
ANY = pl.BlockSpec(memory_space=pltpu.HBM)
TAPS = 9
SLABS = TAPS + (TAPS + 1) // 2
HALF = SLABS // 2
LANES = 128
GROUP = 4
SPAN = 8


def shape(*dims, dtype=BF16):
    return jax.ShapeDtypeStruct(dims, dtype)


def call(body, name, outs, specs, args, scratch=(), limit=16, flops=0, nbytes=0):
    return pl.pallas_call(
        body,
        name=name,
        out_shape=[o for o, _ in outs],
        in_specs=specs,
        out_specs=[s for _, s in outs],
        scratch_shapes=list(scratch),
        compiler_params=pltpu.CompilerParams(vmem_limit_bytes=limit << 20),
        cost_estimate=pl.CostEstimate(flops=flops, bytes_accessed=nbytes, transcendentals=0),
    )(*args)


def to_slab(tap_of, s):
    if s < TAPS:
        return tap_of(s)[:, :LANES]
    first = 2 * (s - TAPS)
    second = min(first + 1, TAPS - 1)
    return jnp.concatenate([tap_of(first)[:, LANES:], tap_of(second)[:, LANES:]], axis=1)


def from_slabs(slab_of, tap):
    tails = slab_of(TAPS + tap // 2)
    half = LANES // 2
    tail = tails[:, half:] if tap % 2 else tails[:, :half]
    return jnp.concatenate([slab_of(tap), tail], axis=1)


def parity():
    return lax.rem(lax.axis_index("lat"), 2)


def pack_body(first, second, half, rest, one, two, sem):
    copies = [
        pltpu.make_async_copy(first, one, sem.at[0]),
        pltpu.make_async_copy(second, two, sem.at[1]),
    ]
    start(copies)
    wait(copies)
    mine = parity() == 0
    for k, kernel in enumerate((one, two)):
        for i in range(HALF):
            low = to_slab(lambda tap: kernel[tap], i)
            high = to_slab(lambda tap: kernel[tap], HALF + i)
            half[k * HALF + i] = jnp.where(mine, low, high)
            rest[k * HALF + i] = jnp.where(mine, high, low)


def ends_body(after, source, upstream, top, bottom, sem):
    del after
    height = source.shape[0]
    copies = []
    for base, rows in ((0, source), (2, upstream)):
        for k, (ref, at) in enumerate(((top, 0), (bottom, height - 2))):
            copies.append(
                pltpu.make_async_copy(
                    rows.at[pl.ds(at, 2)], ref.at[pl.ds(base, 2)], sem.at[base + k]
                )
            )
    start(copies)
    wait(copies)


def gate_body(*refs):
    del refs


def gathered_copies(pieces, own, swapped, other, sem):
    me = lax.axis_index("fsdp")
    count = len(pieces)
    return [
        pltpu.make_async_copy(ref, held.at[me ^ d], sem.at[k * count + d])
        for k, (refs, held) in enumerate(((pieces, own), (swapped, other)))
        for d, ref in enumerate(refs)
    ]


def load_weight(own, other, which, weight, adjoint):
    c = weight.shape[0]
    base = which * HALF
    mine = parity() == 0
    slabs = {}

    def slab(s):
        if s not in slabs:
            side, i = divmod(s, HALF)
            first, second = (own, other) if side == 0 else (other, own)
            parts = [
                jnp.where(mine, first[f, base + i], second[f, base + i])
                for f in range(own.shape[0])
            ]
            slabs[s] = jnp.concatenate(parts, axis=0)
        return slabs[s]

    for tap in range(TAPS):
        value = from_slabs(slab, tap)
        if adjoint:
            weight[:, pl.ds((TAPS - 1 - tap) * c, c)] = value.T
        else:
            weight[:, pl.ds(tap * c, c)] = value


def store_row(columns, at, row):
    c, lon = row.shape
    fill = jnp.zeros((c, columns.shape[2] - lon), row.dtype)
    pieces = (
        jnp.concatenate([row[:, lon - 2 :], row[:, : lon - 2], fill], axis=1),
        jnp.concatenate([row, fill], axis=1),
        jnp.concatenate([row[:, 2:], row[:, :2], fill], axis=1),
    )
    for b, piece in enumerate(pieces):
        columns[at, b * c : (b + 1) * c] = piece


def taps_of(columns, at):
    return jnp.concatenate([columns[at], columns[at + 2], columns[at + 4]], axis=0)


def rows_of(columns, at, count=None):
    return jnp.concatenate([taps_of(columns, at + s) for s in range(count or GROUP)], axis=1)


def chunked(source, target, sem):
    return [
        pltpu.make_async_copy(
            source.at[pl.ds(at, GROUP)], target.at[pl.ds(at, GROUP)], sem.at[at // GROUP]
        )
        for at in range(0, source.shape[0], GROUP)
    ]


def start(copies):
    for copy in copies:
        copy.start()


def wait(copies):
    for copy in copies:
        copy.wait()


def fill(columns, base, rows, lon, lo, hi):
    for r in range(lo, min(hi, rows.shape[0])):
        store_row(columns, r + base, rows[r][:, :lon])


def place_terms(out, base, depth, total, shards, scale, flip):
    c = total.shape[1]
    share = c // shards
    values = {}

    def tap_of(tap):
        if tap not in values:
            if flip:
                values[tap] = total[tap * c : (tap + 1) * c].T * scale
            else:
                values[tap] = total[(TAPS - 1 - tap) * c : (TAPS - tap) * c] * scale
        return values[tap]

    for s in range(SLABS):
        value = to_slab(tap_of, s).astype(BF16)
        for f in range(shards):
            start = s * share
            while start < (s + 1) * share:
                chunk, inside = divmod(start, depth)
                stop = min((s + 1) * share, (chunk + 1) * depth)
                src = f * share + start - s * share
                lo = base + inside
                out[chunk, f, lo : lo + stop - start] = value[src : src + stop - start]
                start = stop


def sum_terms(total, columns, field):
    total[...] = jnp.zeros_like(total)

    def work(t, carry):
        at = t * SPAN
        rhs = jnp.concatenate([field[at + s] for s in range(SPAN)], axis=1)
        total[...] += lax.dot_general(
            rows_of(columns, at, SPAN),
            rhs,
            (((1,), (1,)), ((), ())),
            preferred_element_type=F32,
        )
        return carry

    lax.fori_loop(0, field.shape[0] // SPAN, work, 0)


def stage_body(scale, shards, *refs):
    source, upstream, above_in, below_in = refs[:4]
    pieces, swapped = refs[4 : 4 + shards], refs[4 + shards : 4 + 2 * shards]
    hid, inn, top, bottom, terms = refs[4 + 2 * shards : 9 + 2 * shards]
    (
        src, ups, fcol, ccol, w1, a2, hidden, inner, one, two, above, below, own, other,
        sem, edge_sem, piece_sem,
    ) = refs[9 + 2 * shards :]
    height, _, lon = source.shape
    wide = fcol.shape[2]
    weights = gathered_copies(pieces, own, swapped, other, piece_sem)
    firsts = [
        pltpu.make_async_copy(above_in, above, edge_sem.at[4]),
        pltpu.make_async_copy(below_in, below, edge_sem.at[5]),
    ]
    loads = chunked(source, src, sem.at[0]) + chunked(upstream, ups, sem.at[1])
    start(weights + firsts + loads)
    wait(weights)
    load_weight(own, other, 0, w1, False)
    load_weight(own, other, 1, a2, True)
    wait(firsts + loads)
    for columns, base in ((fcol, 0), (ccol, 2)):
        for r in range(2):
            store_row(columns, r, above[base + r])
            store_row(columns, height + 2 + r, below[base + r])
    fill(fcol, 2, src, lon, 0, GROUP + 2)
    fill(ccol, 2, ups, lon, 0, GROUP + 2)
    saves = [chunked(hidden, hid, sem.at[2]), chunked(inner, inn, sem.at[3])]
    edges = []
    for k, rows in enumerate((hidden, inner)):
        for j, (ref, at) in enumerate(((top, 0), (bottom, height - 2))):
            edges.append(
                pltpu.make_async_copy(
                    rows.at[pl.ds(at, 2)], ref.at[pl.ds(2 * k, 2)], edge_sem.at[2 * k + j]
                )
            )
    for at in range(0, height, GROUP):
        pre = jnp.dot(w1[...], rows_of(fcol, at), preferred_element_type=F32)
        fill(fcol, 2, src, lon, at + GROUP + 2, at + 2 * GROUP + 2)
        back = jnp.dot(a2[...], rows_of(ccol, at), preferred_element_type=F32)
        fill(ccol, 2, ups, lon, at + GROUP + 2, at + 2 * GROUP + 2)
        cdf = 0.5 * (1.0 + lax.erf(pre * 0.7071067811865476))
        value = (pre * cdf).astype(BF16)
        rate = cdf + pre * jnp.exp(-0.5 * pre * pre) * 0.3989422804014327
        grad = (back * rate).astype(BF16)
        for s in range(GROUP):
            hidden[at + s] = value[:, s * wide : (s + 1) * wide]
            inner[at + s] = grad[:, s * wide : (s + 1) * wide]
    start(saves[0] + saves[1] + edges)
    sum_terms(one, fcol, inner)
    sum_terms(two, ccol, hidden)
    depth = terms.shape[2] // 2
    place_terms(terms, 0, depth, one, shards, scale, True)
    place_terms(terms, depth, depth, two, shards, scale, False)
    wait(saves[0] + saves[1] + edges)


def interior_body(shards, *refs):
    source, upstream, hid, inn = refs[:4]
    pieces, swapped = refs[4 : 4 + shards], refs[4 + shards : 4 + 2 * shards]
    out, grad, w2_out, a1_out, token = refs[4 + 2 * shards : 9 + 2 * shards]
    token[...] = jnp.zeros_like(token)
    (
        src, ups, mid, cot, hcol, icol, left, right, w2, a1, own, other,
        sem, weight_sem, piece_sem,
    ) = refs[9 + 2 * shards :]
    height, _, lon = source.shape
    wide = hcol.shape[2]
    firsts = gathered_copies(pieces, own, swapped, other, piece_sem)
    work = (
        (hid, mid, hcol, source, src, w2, left, out),
        (inn, cot, icol, upstream, ups, a1, right, grad),
    )
    loads = [
        chunked(item[0], item[1], sem.at[3 * k]) + chunked(item[3], item[4], sem.at[3 * k + 1])
        for k, item in enumerate(work)
    ]
    start(loads[0][:2] + firsts + loads[0][2:] + loads[1])
    wait(loads[0][:2])
    fill(hcol, 0, mid, lon, 0, 2 * GROUP)
    wait(firsts)
    load_weight(own, other, 1, w2, False)
    load_weight(own, other, 0, a1, True)
    wait(loads[0][2:])
    saves = [
        pltpu.make_async_copy(a, b, weight_sem.at[k])
        for k, (a, b) in enumerate(((w2, w2_out), (a1, a1_out)))
    ]
    start(saves)
    inside = pl.ds(2, height - 4)
    for k, (_, held, columns, _, base, weight, result, target) in enumerate(work):
        for at in range(0, height - 4, GROUP):
            value = jnp.dot(weight[...], rows_of(columns, at), preferred_element_type=F32)
            fill(columns, 0, held, lon, at + 2 * GROUP, at + 3 * GROUP)
            for s in range(GROUP):
                part = value[:, s * wide : s * wide + lon]
                row = at + 2 + s
                result[row] = (base[row].astype(F32) + part).astype(BF16)
        saves.append(
            pltpu.make_async_copy(result.at[inside], target.at[inside], sem.at[3 * k + 2, 0])
        )
        if k == 0:
            wait(loads[1])
            fill(icol, 0, cot, lon, 0, 2 * GROUP)
        saves[-1].start()
    wait(saves)


def edge_body(
    source, upstream, hid, inn, above_in, below_in, w2_in, a1_in, out_in, grad_in,
    out, grad,
    res, mid, columns, result, above, below, w2, a1, sem,
):
    del out_in, grad_in
    firsts = [
        pltpu.make_async_copy(a, b, sem.at[3, k])
        for k, (a, b) in enumerate(
            ((above_in, above), (below_in, below), (w2_in, w2), (a1_in, a1))
        )
    ]
    height, _, lon = source.shape
    wide = columns.shape[3]
    ends = (0, height - 4), (0, height - 2)
    loads, saves = [], []
    for k, (residual, middle, target) in enumerate(((source, hid, out), (upstream, inn, grad))):
        for j in range(2):
            loads.append(
                pltpu.make_async_copy(
                    middle.at[pl.ds(ends[0][j], 4)], mid.at[2 * k + j], sem.at[0, 2 * k + j]
                )
            )
            loads.append(
                pltpu.make_async_copy(
                    residual.at[pl.ds(ends[1][j], 2)], res.at[2 * k + j], sem.at[1, 2 * k + j]
                )
            )
            saves.append(
                pltpu.make_async_copy(
                    result.at[2 * k + j], target.at[pl.ds(ends[1][j], 2)], sem.at[2, 2 * k + j]
                )
            )
    start(firsts[:2] + loads[0:8:2] + firsts[2:] + loads[1:8:2])
    wait(firsts[:2] + loads[0:8:2])
    for k in range(2):
        for r in range(2):
            store_row(columns.at[2 * k], r, above[2 * k + r][:, :lon])
            store_row(columns.at[2 * k + 1], 4 + r, below[2 * k + r][:, :lon])
    wait(firsts[2:] + loads[1:8:2])
    for k, weight in enumerate((w2, a1)):
        for j in range(2):
            for r in range(4):
                store_row(columns.at[2 * k + j], r + 2 - 2 * j, mid[2 * k + j, r][:, :lon])
        rhs = jnp.concatenate(
            [taps_of(columns.at[2 * k + j], r) for j in range(2) for r in range(2)], axis=1
        )
        value = jnp.dot(weight[...], rhs, preferred_element_type=F32)
        for j in range(2):
            for r in range(2):
                lo = (2 * j + r) * wide
                part = value[:, lo : lo + lon]
                base = res[2 * k + j, r].astype(F32)
                result[2 * k + j, r] = (base + part).astype(BF16)
    start(saves)
    wait(saves)


def column_body(got, after, mine, *gives):
    del after
    me = lax.axis_index("fsdp")

    def total(f):
        value = got[0, f].astype(F32)
        for i in range(1, got.shape[0]):
            value += got[i, f].astype(F32)
        return value

    mine[...] = total(me)
    for d, give in enumerate(gives):
        give[...] = total(me ^ (d + 1)).astype(BF16)


def chunk_body(mine, *refs):
    total = mine[...]
    for piece in refs[:-1]:
        total += piece[...].astype(F32)
    for band in range(refs[-1].shape[0]):
        refs[-1][band] = total


def unpack_body(share, depth, chunks, one, two):
    for k, result in enumerate((one, two)):

        def slab(s):
            parts = []
            start = s * share
            while start < (s + 1) * share:
                chunk, inside = divmod(start, depth)
                stop = min((s + 1) * share, (chunk + 1) * depth)
                lo = k * depth + inside
                parts.append(chunks[chunk, lo : lo + stop - start])
                start = stop
            return parts[0] if len(parts) == 1 else jnp.concatenate(parts, axis=0)

        for tap in range(TAPS):
            result[tap] = from_slabs(slab, tap)


def per_device(fields, cotangent, kernel_one, kernel_two):
    _, height, lon, c = fields.shape
    share = kernel_one.shape[3]
    shards = lax.axis_size("fsdp")
    bands = lax.axis_size("lat")
    wide = -(-lon // LANES) * LANES
    scale = 1.0 / (shards * fields.shape[0] * bands * height * lon) ** 0.5
    source = jnp.swapaxes(fields[0], 1, 2)
    upstream = jnp.swapaxes(cotangent[0], 1, 2)
    small = [
        jnp.swapaxes(k.reshape(TAPS, c, share), 1, 2) for k in (kernel_one, kernel_two)
    ]
    forward = [(i, i + 1) for i in range(bands - 1)]
    backward = [(i + 1, i) for i in range(bands - 1)]
    swap = [(i, i ^ 1) for i in range(bands)]

    def edges(top, bottom):
        return lax.ppermute(bottom, "lat", forward), lax.ppermute(top, "lat", backward)

    def partner(value, d):
        return lax.ppermute(value, "fsdp", [(i, i ^ d) for i in range(shards)])

    conv_flops = 2 * TAPS * c * c * height * lon
    groups = height // GROUP
    depth = -(-SLABS * share // (8 * bands)) * 8
    others = range(1, shards)
    slabs = shape(2 * HALF, share, LANES)
    half, rest = call(
        pack_body,
        "pack",
        [(slabs, VMEM), (slabs, VMEM)],
        [ANY, ANY],
        small,
        scratch=[pltpu.VMEM((TAPS, share, c), BF16)] * 2 + [pltpu.SemaphoreType.DMA((2,))],
        limit=60,
    )
    pieces = [partner(half, d) for d in others]
    top, bottom = call(
        ends_body,
        "ends",
        [(shape(4, c, lon), VMEM), (shape(4, c, lon), VMEM)],
        [ANY, ANY, ANY],
        (half, source, upstream),
        scratch=[pltpu.SemaphoreType.DMA((4,))],
        limit=60,
    )
    above, below = edges(top, bottom)
    pieces = pl.pallas_call(
        gate_body,
        name="gate",
        out_shape=[slabs for _ in others],
        in_specs=[ANY] * (shards + 1),
        out_specs=[ANY for _ in others],
        input_output_aliases={i: i for i in range(shards - 1)},
        compiler_params=pltpu.CompilerParams(vmem_limit_bytes=60 << 20),
    )(*pieces, above, below)
    swapped = [lax.ppermute(piece, "lat", swap) for piece in pieces]
    kernels = (half, *pieces, rest, *swapped)

    middle = shape(height, c, wide)
    edge = shape(4, c, wide)
    plain = pltpu.VMEM((height, c, lon), BF16)
    lined = pltpu.VMEM((height, c, wide), BF16)
    columns = pltpu.VMEM((height + 4, 3 * c, wide), BF16)
    matrix = pltpu.VMEM((c, TAPS * c), BF16)
    total = pltpu.VMEM((TAPS * c, c), F32)
    halo = pltpu.VMEM((4, c, lon), BF16)
    gathered = pltpu.VMEM((shards, *slabs.shape), BF16)
    piece_sems = pltpu.SemaphoreType.DMA((2 * shards,))
    hid, inn, top, bottom, terms = call(
        functools.partial(stage_body, scale, shards),
        "stage",
        [
            (middle, ANY),
            (middle, ANY),
            (edge, ANY),
            (edge, ANY),
            (shape(bands, shards, 2 * depth, LANES), VMEM),
        ],
        [ANY] * (4 + 2 * shards),
        (source, upstream, above, below, *kernels),
        scratch=[plain, plain, columns, columns, matrix, matrix, lined, lined, total, total]
        + [halo, halo, gathered, gathered]
        + [pltpu.SemaphoreType.DMA((4, groups)), pltpu.SemaphoreType.DMA((6,)), piece_sems],
        limit=60,
        flops=4 * conv_flops,
        nbytes=1 << 24,
    )
    above, below = edges(top, bottom)
    got = lax.all_to_all(terms, "lat", 0, 0, tiled=True)
    columns = pltpu.VMEM((height, 3 * c, wide), BF16)
    outs = (shape(height, c, lon), ANY)
    weight = (shape(c, TAPS * c), ANY)
    out, grad, w2, a1, token = call(
        functools.partial(interior_body, shards),
        "interior",
        [outs, outs, weight, weight, (shape(8, LANES, dtype=F32), VMEM)],
        [ANY] * (4 + 2 * shards),
        (source, upstream, hid, inn, *kernels),
        scratch=[plain, plain, lined, lined, columns, columns, plain, plain]
        + [matrix, matrix, gathered, gathered]
        + [pltpu.SemaphoreType.DMA((6, groups)), pltpu.SemaphoreType.DMA((2,)), piece_sems],
        limit=60,
        flops=2 * conv_flops,
        nbytes=1 << 24,
    )
    mine, *gives = call(
        column_body,
        "column",
        [(shape(2 * depth, LANES, dtype=F32), VMEM)]
        + [(shape(2 * depth, LANES), VMEM) for _ in others],
        [VMEM, ANY],
        (got, token),
    )
    gains = [partner(give, d) for d, give in zip(others, gives)]
    (chunk,) = call(
        chunk_body,
        "chunk",
        [(shape(bands, 2 * depth, LANES, dtype=F32), VMEM)],
        [VMEM] * shards,
        (mine, *gains),
    )
    chunks = lax.all_to_all(chunk, "lat", 0, 0, tiled=True)
    out, grad = pl.pallas_call(
        edge_body,
        name="edge",
        out_shape=[outs[0], outs[0]],
        in_specs=[ANY] * 10,
        out_specs=[ANY, ANY],
        input_output_aliases={8: 0, 9: 1},
        scratch_shapes=[
            pltpu.VMEM((4, 2, c, lon), BF16),
            pltpu.VMEM((4, 4, c, wide), BF16),
            pltpu.VMEM((4, 6, 3 * c, wide), BF16),
            pltpu.VMEM((4, 2, c, lon), BF16),
            pltpu.VMEM(edge.shape, BF16),
            pltpu.VMEM(edge.shape, BF16),
            matrix,
            matrix,
            pltpu.SemaphoreType.DMA((4, 4)),
        ],
        compiler_params=pltpu.CompilerParams(vmem_limit_bytes=60 << 20),
        cost_estimate=pl.CostEstimate(
            flops=conv_flops // 2, bytes_accessed=1 << 22, transcendentals=0
        ),
    )(source, upstream, hid, inn, above, below, w2, a1, out, grad)
    one, two = call(
        functools.partial(unpack_body, share, depth),
        "unpack",
        [(shape(TAPS, share, c, dtype=F32), VMEM)] * 2,
        [VMEM],
        (chunks,),
    )
    return (
        jnp.swapaxes(out, 1, 2)[None],
        jnp.swapaxes(grad, 1, 2)[None],
        jnp.swapaxes(one, 1, 2).reshape(3, 3, c, share),
        jnp.swapaxes(two, 1, 2).reshape(3, 3, c, share),
    )


def solution(mesh):
    placed = (
        P("fsdp", "lat", None, None),
        P("fsdp", "lat", None, None),
        P(None, None, None, "fsdp"),
        P(None, None, None, "fsdp"),
    )
    return jax.shard_map(
        per_device,
        mesh=mesh,
        in_specs=placed,
        out_specs=placed,
        check_vma=False,
    )
```

```python
import functools

import jax
import jax.numpy as jnp
from jax import lax
from jax.experimental import pallas as pl
from jax.experimental.pallas import tpu as pltpu
from jax.sharding import PartitionSpec as P

BF16 = jnp.bfloat16
F32 = jnp.float32
VMEM = pl.BlockSpec(memory_space=pltpu.VMEM)
ANY = pl.BlockSpec(memory_space=pltpu.HBM)
TAPS = 9
SLABS = TAPS + (TAPS + 1) // 2
HALF = SLABS // 2
LANES = 128
GROUP = 4
SPAN = 8
SWEEP = 8


def shape(*dims, dtype=BF16):
    return jax.ShapeDtypeStruct(dims, dtype)


def call(body, name, outs, specs, args, scratch=(), limit=16, flops=0, nbytes=0):
    return pl.pallas_call(
        body,
        name=name,
        out_shape=[o for o, _ in outs],
        in_specs=specs,
        out_specs=[s for _, s in outs],
        scratch_shapes=list(scratch),
        compiler_params=pltpu.CompilerParams(vmem_limit_bytes=limit << 20),
        cost_estimate=pl.CostEstimate(flops=flops, bytes_accessed=nbytes, transcendentals=0),
    )(*args)


def to_slab(tap_of, s):
    if s < TAPS:
        return tap_of(s)[:, :LANES]
    first = 2 * (s - TAPS)
    second = min(first + 1, TAPS - 1)
    return jnp.concatenate([tap_of(first)[:, LANES:], tap_of(second)[:, LANES:]], axis=1)


def from_slabs(slab_of, tap):
    tails = slab_of(TAPS + tap // 2)
    half = LANES // 2
    tail = tails[:, half:] if tap % 2 else tails[:, :half]
    return jnp.concatenate([slab_of(tap), tail], axis=1)


def parity():
    return lax.rem(lax.axis_index("lat"), 2)


def pack_body(first, second, half, rest, one, two, sem):
    copies = [
        pltpu.make_async_copy(first, one, sem.at[0]),
        pltpu.make_async_copy(second, two, sem.at[1]),
    ]
    start(copies)
    wait(copies)
    mine = parity() == 0
    for k, kernel in enumerate((one, two)):
        for i in range(HALF):
            low = to_slab(lambda tap: kernel[tap], i)
            high = to_slab(lambda tap: kernel[tap], HALF + i)
            half[k * HALF + i] = jnp.where(mine, low, high)
            rest[k * HALF + i] = jnp.where(mine, high, low)


def ends_body(after, source, upstream, top, bottom, sem):
    del after
    height = source.shape[0]
    copies = []
    for base, rows in ((0, source), (2, upstream)):
        for k, (ref, at) in enumerate(((top, 0), (bottom, height - 2))):
            copies.append(
                pltpu.make_async_copy(
                    rows.at[pl.ds(at, 2)], ref.at[pl.ds(base, 2)], sem.at[base + k]
                )
            )
    start(copies)
    wait(copies)


def gate_body(*refs):
    del refs


def gathered_copies(pieces, own, swapped, other, sem):
    me = lax.axis_index("fsdp")
    count = len(pieces)
    return [
        pltpu.make_async_copy(ref, held.at[me ^ d], sem.at[k * count + d])
        for k, (refs, held) in enumerate(((pieces, own), (swapped, other)))
        for d, ref in enumerate(refs)
    ]


def load_weight(own, other, which, weight, adjoint):
    c = weight.shape[0]
    base = which * HALF
    mine = parity() == 0
    slabs = {}

    def slab(s):
        if s not in slabs:
            side, i = divmod(s, HALF)
            first, second = (own, other) if side == 0 else (other, own)
            parts = [
                jnp.where(mine, first[f, base + i], second[f, base + i])
                for f in range(own.shape[0])
            ]
            slabs[s] = jnp.concatenate(parts, axis=0)
        return slabs[s]

    for tap in range(TAPS):
        value = from_slabs(slab, tap)
        if adjoint:
            weight[:, pl.ds((TAPS - 1 - tap) * c, c)] = value.T
        else:
            weight[:, pl.ds(tap * c, c)] = value


def store_row(columns, at, row):
    c, lon = row.shape
    fill = jnp.zeros((c, columns.shape[2] - lon), row.dtype)
    pieces = (
        jnp.concatenate([row[:, lon - 2 :], row[:, : lon - 2], fill], axis=1),
        jnp.concatenate([row, fill], axis=1),
        jnp.concatenate([row[:, 2:], row[:, :2], fill], axis=1),
    )
    for b, piece in enumerate(pieces):
        columns[at, b * c : (b + 1) * c] = piece


def taps_of(columns, at):
    return jnp.concatenate([columns[at], columns[at + 2], columns[at + 4]], axis=0)


def rows_of(columns, at, count=None):
    return jnp.concatenate([taps_of(columns, at + s) for s in range(count or GROUP)], axis=1)


def chunked(source, target, sem):
    return [
        pltpu.make_async_copy(
            source.at[pl.ds(at, GROUP)], target.at[pl.ds(at, GROUP)], sem.at[at // GROUP]
        )
        for at in range(0, source.shape[0], GROUP)
    ]


def start(copies):
    for copy in copies:
        copy.start()


def wait(copies):
    for copy in copies:
        copy.wait()


def fill(columns, base, rows, lon, lo, hi):
    for r in range(lo, min(hi, rows.shape[0])):
        store_row(columns, r + base, rows[r][:, :lon])


def place_terms(out, base, depth, total, shards, scale, flip):
    c = total.shape[1]
    share = c // shards
    values = {}

    def tap_of(tap):
        if tap not in values:
            if flip:
                values[tap] = total[tap * c : (tap + 1) * c].T * scale
            else:
                values[tap] = total[(TAPS - 1 - tap) * c : (TAPS - tap) * c] * scale
        return values[tap]

    for s in range(SLABS):
        value = to_slab(tap_of, s).astype(BF16)
        for f in range(shards):
            start = s * share
            while start < (s + 1) * share:
                chunk, inside = divmod(start, depth)
                stop = min((s + 1) * share, (chunk + 1) * depth)
                src = f * share + start - s * share
                lo = base + inside
                out[chunk, f, lo : lo + stop - start] = value[src : src + stop - start]
                start = stop


def sum_terms(total, columns, field):
    total[...] = jnp.zeros_like(total)

    def work(t, carry):
        at = t * SPAN
        rhs = jnp.concatenate([field[at + s] for s in range(SPAN)], axis=1)
        total[...] += lax.dot_general(
            rows_of(columns, at, SPAN),
            rhs,
            (((1,), (1,)), ((), ())),
            preferred_element_type=F32,
        )
        return carry

    lax.fori_loop(0, field.shape[0] // SPAN, work, 0)


def stage_body(scale, shards, *refs):
    source, upstream, above_in, below_in = refs[:4]
    pieces, swapped = refs[4 : 4 + shards], refs[4 + shards : 4 + 2 * shards]
    hid, inn, top, bottom, terms = refs[4 + 2 * shards : 9 + 2 * shards]
    (
        src, ups, fcol, ccol, w1, a2, hidden, inner, one, two, above, below, own, other,
        sem, edge_sem, piece_sem,
    ) = refs[9 + 2 * shards :]
    height, _, lon = source.shape
    wide = fcol.shape[2]
    weights = gathered_copies(pieces, own, swapped, other, piece_sem)
    firsts = [
        pltpu.make_async_copy(above_in, above, edge_sem.at[4]),
        pltpu.make_async_copy(below_in, below, edge_sem.at[5]),
    ]
    loads = chunked(source, src, sem.at[0]) + chunked(upstream, ups, sem.at[1])
    start(weights + firsts + loads)
    wait(weights)
    load_weight(own, other, 0, w1, False)
    load_weight(own, other, 1, a2, True)
    wait(firsts + loads)
    for columns, base in ((fcol, 0), (ccol, 2)):
        for r in range(2):
            store_row(columns, r, above[base + r])
            store_row(columns, height + 2 + r, below[base + r])
    fill(fcol, 2, src, lon, 0, SWEEP + 2)
    fill(ccol, 2, ups, lon, 0, SWEEP + 2)
    saves = [chunked(hidden, hid, sem.at[2]), chunked(inner, inn, sem.at[3])]
    edges = []
    for k, rows in enumerate((hidden, inner)):
        for j, (ref, at) in enumerate(((top, 0), (bottom, height - 2))):
            edges.append(
                pltpu.make_async_copy(
                    rows.at[pl.ds(at, 2)], ref.at[pl.ds(2 * k, 2)], edge_sem.at[2 * k + j]
                )
            )
    for at in range(0, height, SWEEP):
        pre = jnp.dot(w1[...], rows_of(fcol, at, SWEEP), preferred_element_type=F32)
        fill(fcol, 2, src, lon, at + SWEEP + 2, at + 2 * SWEEP + 2)
        back = jnp.dot(a2[...], rows_of(ccol, at, SWEEP), preferred_element_type=F32)
        fill(ccol, 2, ups, lon, at + SWEEP + 2, at + 2 * SWEEP + 2)
        cdf = 0.5 * (1.0 + lax.erf(pre * 0.7071067811865476))
        value = (pre * cdf).astype(BF16)
        rate = cdf + pre * jnp.exp(-0.5 * pre * pre) * 0.3989422804014327
        grad = (back * rate).astype(BF16)
        for s in range(SWEEP):
            hidden[at + s] = value[:, s * wide : (s + 1) * wide]
            inner[at + s] = grad[:, s * wide : (s + 1) * wide]
    start(saves[0] + saves[1] + edges)
    sum_terms(one, fcol, inner)
    sum_terms(two, ccol, hidden)
    depth = terms.shape[2] // 2
    place_terms(terms, 0, depth, one, shards, scale, True)
    place_terms(terms, depth, depth, two, shards, scale, False)
    wait(saves[0] + saves[1] + edges)


def interior_body(shards, *refs):
    source, upstream, hid, inn = refs[:4]
    pieces, swapped = refs[4 : 4 + shards], refs[4 + shards : 4 + 2 * shards]
    out, grad, w2_out, a1_out, token = refs[4 + 2 * shards : 9 + 2 * shards]
    token[...] = jnp.zeros_like(token)
    (
        src, ups, mid, cot, hcol, icol, left, right, w2, a1, own, other,
        sem, weight_sem, piece_sem,
    ) = refs[9 + 2 * shards :]
    height, _, lon = source.shape
    wide = hcol.shape[2]
    firsts = gathered_copies(pieces, own, swapped, other, piece_sem)
    work = (
        (hid, mid, hcol, source, src, w2, left, out),
        (inn, cot, icol, upstream, ups, a1, right, grad),
    )
    loads = [
        chunked(item[0], item[1], sem.at[3 * k]) + chunked(item[3], item[4], sem.at[3 * k + 1])
        for k, item in enumerate(work)
    ]
    start(loads[0][:2] + firsts + loads[0][2:] + loads[1])
    wait(loads[0][:2])
    fill(hcol, 0, mid, lon, 0, 2 * GROUP)
    wait(firsts)
    load_weight(own, other, 1, w2, False)
    load_weight(own, other, 0, a1, True)
    wait(loads[0][2:])
    saves = [
        pltpu.make_async_copy(a, b, weight_sem.at[k])
        for k, (a, b) in enumerate(((w2, w2_out), (a1, a1_out)))
    ]
    start(saves)
    inside = pl.ds(2, height - 4)
    for k, (_, held, columns, _, base, weight, result, target) in enumerate(work):
        for at in range(0, height - 4, GROUP):
            value = jnp.dot(weight[...], rows_of(columns, at), preferred_element_type=F32)
            fill(columns, 0, held, lon, at + 2 * GROUP, at + 3 * GROUP)
            for s in range(GROUP):
                part = value[:, s * wide : s * wide + lon]
                row = at + 2 + s
                result[row] = (base[row].astype(F32) + part).astype(BF16)
        saves.append(
            pltpu.make_async_copy(result.at[inside], target.at[inside], sem.at[3 * k + 2, 0])
        )
        if k == 0:
            wait(loads[1])
            fill(icol, 0, cot, lon, 0, 2 * GROUP)
        saves[-1].start()
    wait(saves)


def edge_body(
    source, upstream, hid, inn, above_in, below_in, w2_in, a1_in, out_in, grad_in,
    out, grad,
    res, mid, columns, result, above, below, w2, a1, sem,
):
    del out_in, grad_in
    firsts = [
        pltpu.make_async_copy(a, b, sem.at[3, k])
        for k, (a, b) in enumerate(
            ((above_in, above), (below_in, below), (w2_in, w2), (a1_in, a1))
        )
    ]
    height, _, lon = source.shape
    wide = columns.shape[3]
    ends = (0, height - 4), (0, height - 2)
    loads, saves = [], []
    for k, (residual, middle, target) in enumerate(((source, hid, out), (upstream, inn, grad))):
        for j in range(2):
            loads.append(
                pltpu.make_async_copy(
                    middle.at[pl.ds(ends[0][j], 4)], mid.at[2 * k + j], sem.at[0, 2 * k + j]
                )
            )
            loads.append(
                pltpu.make_async_copy(
                    residual.at[pl.ds(ends[1][j], 2)], res.at[2 * k + j], sem.at[1, 2 * k + j]
                )
            )
            saves.append(
                pltpu.make_async_copy(
                    result.at[2 * k + j], target.at[pl.ds(ends[1][j], 2)], sem.at[2, 2 * k + j]
                )
            )
    start(firsts[:2] + loads[0:8:2] + firsts[2:] + loads[1:8:2])
    wait(firsts[:2] + loads[0:8:2])
    for k in range(2):
        for r in range(2):
            store_row(columns.at[2 * k], r, above[2 * k + r][:, :lon])
            store_row(columns.at[2 * k + 1], 4 + r, below[2 * k + r][:, :lon])
    wait(firsts[2:] + loads[1:8:2])
    for k, weight in enumerate((w2, a1)):
        for j in range(2):
            for r in range(4):
                store_row(columns.at[2 * k + j], r + 2 - 2 * j, mid[2 * k + j, r][:, :lon])
        rhs = jnp.concatenate(
            [taps_of(columns.at[2 * k + j], r) for j in range(2) for r in range(2)], axis=1
        )
        value = jnp.dot(weight[...], rhs, preferred_element_type=F32)
        for j in range(2):
            for r in range(2):
                lo = (2 * j + r) * wide
                part = value[:, lo : lo + lon]
                base = res[2 * k + j, r].astype(F32)
                result[2 * k + j, r] = (base + part).astype(BF16)
    start(saves)
    wait(saves)


def column_body(got, after, mine, *gives):
    del after
    me = lax.axis_index("fsdp")

    def total(f):
        value = got[0, f].astype(F32)
        for i in range(1, got.shape[0]):
            value += got[i, f].astype(F32)
        return value

    mine[...] = total(me)
    for d, give in enumerate(gives):
        give[...] = total(me ^ (d + 1)).astype(BF16)


def chunk_body(mine, *refs):
    total = mine[...]
    for piece in refs[:-1]:
        total += piece[...].astype(F32)
    for band in range(refs[-1].shape[0]):
        refs[-1][band] = total


def unpack_body(share, depth, chunks, one, two):
    for k, result in enumerate((one, two)):

        def slab(s):
            parts = []
            start = s * share
            while start < (s + 1) * share:
                chunk, inside = divmod(start, depth)
                stop = min((s + 1) * share, (chunk + 1) * depth)
                lo = k * depth + inside
                parts.append(chunks[chunk, lo : lo + stop - start])
                start = stop
            return parts[0] if len(parts) == 1 else jnp.concatenate(parts, axis=0)

        for tap in range(TAPS):
            result[tap] = from_slabs(slab, tap)


def per_device(fields, cotangent, kernel_one, kernel_two):
    _, height, lon, c = fields.shape
    share = kernel_one.shape[3]
    shards = lax.axis_size("fsdp")
    bands = lax.axis_size("lat")
    wide = -(-lon // LANES) * LANES
    scale = 1.0 / (shards * fields.shape[0] * bands * height * lon) ** 0.5
    source = jnp.swapaxes(fields[0], 1, 2)
    upstream = jnp.swapaxes(cotangent[0], 1, 2)
    small = [
        jnp.swapaxes(k.reshape(TAPS, c, share), 1, 2) for k in (kernel_one, kernel_two)
    ]
    forward = [(i, i + 1) for i in range(bands - 1)]
    backward = [(i + 1, i) for i in range(bands - 1)]
    swap = [(i, i ^ 1) for i in range(bands)]

    def edges(top, bottom):
        return lax.ppermute(bottom, "lat", forward), lax.ppermute(top, "lat", backward)

    def partner(value, d):
        return lax.ppermute(value, "fsdp", [(i, i ^ d) for i in range(shards)])

    conv_flops = 2 * TAPS * c * c * height * lon
    groups = height // GROUP
    depth = -(-SLABS * share // (8 * bands)) * 8
    others = range(1, shards)
    slabs = shape(2 * HALF, share, LANES)
    half, rest = call(
        pack_body,
        "pack",
        [(slabs, VMEM), (slabs, VMEM)],
        [ANY, ANY],
        small,
        scratch=[pltpu.VMEM((TAPS, share, c), BF16)] * 2 + [pltpu.SemaphoreType.DMA((2,))],
        limit=60,
    )
    pieces = [partner(half, d) for d in others]
    top, bottom = call(
        ends_body,
        "ends",
        [(shape(4, c, lon), VMEM), (shape(4, c, lon), VMEM)],
        [ANY, ANY, ANY],
        (half, source, upstream),
        scratch=[pltpu.SemaphoreType.DMA((4,))],
        limit=60,
    )
    above, below = edges(top, bottom)
    pieces = pl.pallas_call(
        gate_body,
        name="gate",
        out_shape=[slabs for _ in others],
        in_specs=[VMEM] * (shards + 1),
        out_specs=[VMEM for _ in others],
        input_output_aliases={i: i for i in range(shards - 1)},
        compiler_params=pltpu.CompilerParams(vmem_limit_bytes=16 << 20),
    )(*pieces, above, below)
    swapped = [lax.ppermute(piece, "lat", swap) for piece in pieces]
    kernels = (half, *pieces, rest, *swapped)

    middle = shape(height, c, wide)
    edge = shape(4, c, wide)
    plain = pltpu.VMEM((height, c, lon), BF16)
    lined = pltpu.VMEM((height, c, wide), BF16)
    columns = pltpu.VMEM((height + 4, 3 * c, wide), BF16)
    matrix = pltpu.VMEM((c, TAPS * c), BF16)
    total = pltpu.VMEM((TAPS * c, c), F32)
    halo = pltpu.VMEM((4, c, lon), BF16)
    gathered = pltpu.VMEM((shards, *slabs.shape), BF16)
    piece_sems = pltpu.SemaphoreType.DMA((2 * shards,))
    hid, inn, top, bottom, terms = call(
        functools.partial(stage_body, scale, shards),
        "stage",
        [
            (middle, ANY),
            (middle, ANY),
            (edge, ANY),
            (edge, ANY),
            (shape(bands, shards, 2 * depth, LANES), VMEM),
        ],
        [ANY] * (4 + 2 * shards),
        (source, upstream, above, below, *kernels),
        scratch=[plain, plain, columns, columns, matrix, matrix, lined, lined, total, total]
        + [halo, halo, gathered, gathered]
        + [pltpu.SemaphoreType.DMA((4, groups)), pltpu.SemaphoreType.DMA((6,)), piece_sems],
        limit=60,
        flops=4 * conv_flops,
        nbytes=1 << 24,
    )
    above, below = edges(top, bottom)
    got = lax.all_to_all(terms, "lat", 0, 0, tiled=True)
    columns = pltpu.VMEM((height, 3 * c, wide), BF16)
    outs = (shape(height, c, lon), ANY)
    weight = (shape(c, TAPS * c), ANY)
    out, grad, w2, a1, token = call(
        functools.partial(interior_body, shards),
        "interior",
        [outs, outs, weight, weight, (shape(8, LANES, dtype=F32), VMEM)],
        [ANY] * (4 + 2 * shards),
        (source, upstream, hid, inn, *kernels),
        scratch=[plain, plain, lined, lined, columns, columns, plain, plain]
        + [matrix, matrix, gathered, gathered]
        + [pltpu.SemaphoreType.DMA((6, groups)), pltpu.SemaphoreType.DMA((2,)), piece_sems],
        limit=60,
        flops=2 * conv_flops,
        nbytes=1 << 24,
    )
    mine, *gives = call(
        column_body,
        "column",
        [(shape(2 * depth, LANES, dtype=F32), VMEM)]
        + [(shape(2 * depth, LANES), VMEM) for _ in others],
        [VMEM, VMEM],
        (got, token),
    )
    gains = [partner(give, d) for d, give in zip(others, gives)]
    (chunk,) = call(
        chunk_body,
        "chunk",
        [(shape(bands, 2 * depth, LANES, dtype=F32), VMEM)],
        [VMEM] * shards,
        (mine, *gains),
    )
    chunks = lax.all_to_all(chunk, "lat", 0, 0, tiled=True)
    out, grad = pl.pallas_call(
        edge_body,
        name="edge",
        out_shape=[outs[0], outs[0]],
        in_specs=[ANY] * 10,
        out_specs=[ANY, ANY],
        input_output_aliases={8: 0, 9: 1},
        scratch_shapes=[
            pltpu.VMEM((4, 2, c, lon), BF16),
            pltpu.VMEM((4, 4, c, wide), BF16),
            pltpu.VMEM((4, 6, 3 * c, wide), BF16),
            pltpu.VMEM((4, 2, c, lon), BF16),
            pltpu.VMEM(edge.shape, BF16),
            pltpu.VMEM(edge.shape, BF16),
            matrix,
            matrix,
            pltpu.SemaphoreType.DMA((4, 4)),
        ],
        compiler_params=pltpu.CompilerParams(vmem_limit_bytes=60 << 20),
        cost_estimate=pl.CostEstimate(
            flops=conv_flops // 2, bytes_accessed=1 << 22, transcendentals=0
        ),
    )(source, upstream, hid, inn, above, below, w2, a1, out, grad)
    one, two = call(
        functools.partial(unpack_body, share, depth),
        "unpack",
        [(shape(TAPS, share, c, dtype=F32), VMEM)] * 2,
        [VMEM],
        (chunks,),
    )
    return (
        jnp.swapaxes(out, 1, 2)[None],
        jnp.swapaxes(grad, 1, 2)[None],
        jnp.swapaxes(one, 1, 2).reshape(3, 3, c, share),
        jnp.swapaxes(two, 1, 2).reshape(3, 3, c, share),
    )


def solution(mesh):
    placed = (
        P("fsdp", "lat", None, None),
        P("fsdp", "lat", None, None),
        P(None, None, None, "fsdp"),
        P(None, None, None, "fsdp"),
    )
    return jax.shard_map(
        per_device,
        mesh=mesh,
        in_specs=placed,
        out_specs=placed,
        check_vma=False,
    )
```

```python
import functools

import jax
import jax.numpy as jnp
from jax import lax
from jax.experimental import pallas as pl
from jax.experimental.pallas import tpu as pltpu
from jax.sharding import PartitionSpec as P

BF16 = jnp.bfloat16
F32 = jnp.float32
VMEM = pl.BlockSpec(memory_space=pltpu.VMEM)
ANY = pl.BlockSpec(memory_space=pltpu.HBM)
TAPS = 9
SLABS = TAPS + (TAPS + 1) // 2
HALF = SLABS // 2
LANES = 128
GROUP = 4
SPAN = 8
SWEEP = 8


def shape(*dims, dtype=BF16):
    return jax.ShapeDtypeStruct(dims, dtype)


def call(body, name, outs, specs, args, scratch=(), limit=16, flops=0, nbytes=0):
    return pl.pallas_call(
        body,
        name=name,
        out_shape=[o for o, _ in outs],
        in_specs=specs,
        out_specs=[s for _, s in outs],
        scratch_shapes=list(scratch),
        compiler_params=pltpu.CompilerParams(vmem_limit_bytes=limit << 20),
        cost_estimate=pl.CostEstimate(flops=flops, bytes_accessed=nbytes, transcendentals=0),
    )(*args)


def to_slab(tap_of, s):
    if s < TAPS:
        return tap_of(s)[:, :LANES]
    first = 2 * (s - TAPS)
    second = min(first + 1, TAPS - 1)
    return jnp.concatenate([tap_of(first)[:, LANES:], tap_of(second)[:, LANES:]], axis=1)


def from_slabs(slab_of, tap):
    tails = slab_of(TAPS + tap // 2)
    half = LANES // 2
    tail = tails[:, half:] if tap % 2 else tails[:, :half]
    return jnp.concatenate([slab_of(tap), tail], axis=1)


def parity():
    return lax.rem(lax.axis_index("lat"), 2)


def pack_body(first, second, source, upstream, half, rest, top, bottom, one, two, sem):
    height = source.shape[0]
    copies = [
        pltpu.make_async_copy(first, one, sem.at[4]),
        pltpu.make_async_copy(second, two, sem.at[5]),
    ]
    for base, rows in ((0, source), (2, upstream)):
        for k, (ref, at) in enumerate(((top, 0), (bottom, height - 2))):
            copies.append(
                pltpu.make_async_copy(
                    rows.at[pl.ds(at, 2)], ref.at[pl.ds(base, 2)], sem.at[base + k]
                )
            )
    start(copies)
    wait(copies[:2])
    mine = parity() == 0
    for k, kernel in enumerate((one, two)):
        for i in range(HALF):
            low = to_slab(lambda tap: kernel[tap], i)
            high = to_slab(lambda tap: kernel[tap], HALF + i)
            half[k * HALF + i] = jnp.where(mine, low, high)
            rest[k * HALF + i] = jnp.where(mine, high, low)
    wait(copies[2:])


def gate_body(*refs):
    del refs


def gathered_copies(pieces, own, swapped, other, sem):
    me = lax.axis_index("fsdp")
    count = len(pieces)
    return [
        pltpu.make_async_copy(ref, held.at[me ^ d], sem.at[k * count + d])
        for k, (refs, held) in enumerate(((pieces, own), (swapped, other)))
        for d, ref in enumerate(refs)
    ]


def load_weight(own, other, which, weight, adjoint):
    c = weight.shape[0]
    base = which * HALF
    mine = parity() == 0
    slabs = {}

    def slab(s):
        if s not in slabs:
            side, i = divmod(s, HALF)
            first, second = (own, other) if side == 0 else (other, own)
            parts = [
                jnp.where(mine, first[f, base + i], second[f, base + i])
                for f in range(own.shape[0])
            ]
            slabs[s] = jnp.concatenate(parts, axis=0)
        return slabs[s]

    for tap in range(TAPS):
        value = from_slabs(slab, tap)
        if adjoint:
            weight[:, pl.ds((TAPS - 1 - tap) * c, c)] = value.T
        else:
            weight[:, pl.ds(tap * c, c)] = value


def store_row(columns, at, row):
    c, lon = row.shape
    fill = jnp.zeros((c, columns.shape[2] - lon), row.dtype)
    pieces = (
        jnp.concatenate([row[:, lon - 2 :], row[:, : lon - 2], fill], axis=1),
        jnp.concatenate([row, fill], axis=1),
        jnp.concatenate([row[:, 2:], row[:, :2], fill], axis=1),
    )
    for b, piece in enumerate(pieces):
        columns[at, b * c : (b + 1) * c] = piece


def taps_of(columns, at):
    return jnp.concatenate([columns[at], columns[at + 2], columns[at + 4]], axis=0)


def rows_of(columns, at, count=None):
    return jnp.concatenate([taps_of(columns, at + s) for s in range(count or GROUP)], axis=1)


def chunked(source, target, sem):
    return [
        pltpu.make_async_copy(
            source.at[pl.ds(at, GROUP)], target.at[pl.ds(at, GROUP)], sem.at[at // GROUP]
        )
        for at in range(0, source.shape[0], GROUP)
    ]


def start(copies):
    for copy in copies:
        copy.start()


def wait(copies):
    for copy in copies:
        copy.wait()


def fill(columns, base, rows, lon, lo, hi):
    for r in range(lo, min(hi, rows.shape[0])):
        store_row(columns, r + base, rows[r][:, :lon])


def place_terms(out, base, depth, total, shards, scale, flip):
    c = total.shape[1]
    share = c // shards
    values = {}

    def tap_of(tap):
        if tap not in values:
            if flip:
                values[tap] = total[tap * c : (tap + 1) * c].T * scale
            else:
                values[tap] = total[(TAPS - 1 - tap) * c : (TAPS - tap) * c] * scale
        return values[tap]

    for s in range(SLABS):
        value = to_slab(tap_of, s).astype(BF16)
        for f in range(shards):
            start = s * share
            while start < (s + 1) * share:
                chunk, inside = divmod(start, depth)
                stop = min((s + 1) * share, (chunk + 1) * depth)
                src = f * share + start - s * share
                lo = base + inside
                out[chunk, f, lo : lo + stop - start] = value[src : src + stop - start]
                start = stop


def sum_terms(total, columns, field):
    total[...] = jnp.zeros_like(total)

    def work(t, carry):
        at = t * SPAN
        rhs = jnp.concatenate([field[at + s] for s in range(SPAN)], axis=1)
        total[...] += lax.dot_general(
            rows_of(columns, at, SPAN),
            rhs,
            (((1,), (1,)), ((), ())),
            preferred_element_type=F32,
        )
        return carry

    lax.fori_loop(0, field.shape[0] // SPAN, work, 0)


def stage_body(scale, shards, *refs):
    source, upstream, above_in, below_in = refs[:4]
    pieces, swapped = refs[4 : 4 + shards], refs[4 + shards : 4 + 2 * shards]
    hid, inn, top, bottom, terms = refs[4 + 2 * shards : 9 + 2 * shards]
    (
        src, ups, fcol, ccol, w1, a2, hidden, inner, one, two, above, below, own, other,
        sem, edge_sem, piece_sem,
    ) = refs[9 + 2 * shards :]
    height, _, lon = source.shape
    wide = fcol.shape[2]
    weights = gathered_copies(pieces, own, swapped, other, piece_sem)
    firsts = [
        pltpu.make_async_copy(above_in, above, edge_sem.at[4]),
        pltpu.make_async_copy(below_in, below, edge_sem.at[5]),
    ]
    loads = chunked(source, src, sem.at[0]) + chunked(upstream, ups, sem.at[1])
    start(weights + firsts + loads)
    wait(weights)
    load_weight(own, other, 0, w1, False)
    load_weight(own, other, 1, a2, True)
    wait(firsts + loads)
    for columns, base in ((fcol, 0), (ccol, 2)):
        for r in range(2):
            store_row(columns, r, above[base + r])
            store_row(columns, height + 2 + r, below[base + r])
    fill(fcol, 2, src, lon, 0, SWEEP + 2)
    fill(ccol, 2, ups, lon, 0, SWEEP + 2)
    saves = [chunked(hidden, hid, sem.at[2]), chunked(inner, inn, sem.at[3])]
    edges = []
    for k, rows in enumerate((hidden, inner)):
        for j, (ref, at) in enumerate(((top, 0), (bottom, height - 2))):
            edges.append(
                pltpu.make_async_copy(
                    rows.at[pl.ds(at, 2)], ref.at[pl.ds(2 * k, 2)], edge_sem.at[2 * k + j]
                )
            )
    for at in range(0, height, SWEEP):
        pre = jnp.dot(w1[...], rows_of(fcol, at, SWEEP), preferred_element_type=F32)
        fill(fcol, 2, src, lon, at + SWEEP + 2, at + 2 * SWEEP + 2)
        back = jnp.dot(a2[...], rows_of(ccol, at, SWEEP), preferred_element_type=F32)
        fill(ccol, 2, ups, lon, at + SWEEP + 2, at + 2 * SWEEP + 2)
        cdf = 0.5 * (1.0 + lax.erf(pre * 0.7071067811865476))
        value = (pre * cdf).astype(BF16)
        rate = cdf + pre * jnp.exp(-0.5 * pre * pre) * 0.3989422804014327
        grad = (back * rate).astype(BF16)
        for s in range(SWEEP):
            hidden[at + s] = value[:, s * wide : (s + 1) * wide]
            inner[at + s] = grad[:, s * wide : (s + 1) * wide]
    start(saves[0] + saves[1] + edges)
    sum_terms(one, fcol, inner)
    sum_terms(two, ccol, hidden)
    depth = terms.shape[2] // 2
    place_terms(terms, 0, depth, one, shards, scale, True)
    place_terms(terms, depth, depth, two, shards, scale, False)
    wait(saves[0] + saves[1] + edges)


def interior_body(shards, *refs):
    source, upstream, hid, inn = refs[:4]
    pieces, swapped = refs[4 : 4 + shards], refs[4 + shards : 4 + 2 * shards]
    out, grad, w2_out, a1_out, token = refs[4 + 2 * shards : 9 + 2 * shards]
    token[...] = jnp.zeros_like(token)
    (
        src, ups, mid, cot, hcol, icol, left, right, w2, a1, own, other,
        sem, weight_sem, piece_sem,
    ) = refs[9 + 2 * shards :]
    height, _, lon = source.shape
    wide = hcol.shape[2]
    firsts = gathered_copies(pieces, own, swapped, other, piece_sem)
    work = (
        (hid, mid, hcol, source, src, w2, left, out),
        (inn, cot, icol, upstream, ups, a1, right, grad),
    )
    loads = [
        chunked(item[0], item[1], sem.at[3 * k]) + chunked(item[3], item[4], sem.at[3 * k + 1])
        for k, item in enumerate(work)
    ]
    start(loads[0][:2] + firsts + loads[0][2:] + loads[1])
    wait(loads[0][:2])
    fill(hcol, 0, mid, lon, 0, 2 * GROUP)
    wait(firsts)
    load_weight(own, other, 1, w2, False)
    load_weight(own, other, 0, a1, True)
    wait(loads[0][2:])
    saves = [
        pltpu.make_async_copy(a, b, weight_sem.at[k])
        for k, (a, b) in enumerate(((w2, w2_out), (a1, a1_out)))
    ]
    start(saves)
    inside = pl.ds(2, height - 4)
    stride = (height - 4) // 2
    for k, (_, held, columns, _, base, weight, result, target) in enumerate(work):
        for at in range(0, height - 4, stride):
            if at == 0:
                fill(columns, 0, held, lon, 2 * GROUP, stride + 4)
            value = jnp.dot(weight[...], rows_of(columns, at, stride), preferred_element_type=F32)
            fill(columns, 0, held, lon, at + stride + 4, at + 2 * stride + 4)
            for s in range(stride):
                part = value[:, s * wide : s * wide + lon]
                row = at + 2 + s
                result[row] = (base[row].astype(F32) + part).astype(BF16)
        saves.append(
            pltpu.make_async_copy(result.at[inside], target.at[inside], sem.at[3 * k + 2, 0])
        )
        if k == 0:
            wait(loads[1])
            fill(icol, 0, cot, lon, 0, 2 * GROUP)
        saves[-1].start()
    wait(saves)


def edge_body(
    source, upstream, hid, inn, above_in, below_in, w2_in, a1_in, out_in, grad_in,
    out, grad,
    res, mid, columns, result, above, below, w2, a1, sem,
):
    del out_in, grad_in
    firsts = [
        pltpu.make_async_copy(a, b, sem.at[3, k])
        for k, (a, b) in enumerate(
            ((above_in, above), (below_in, below), (w2_in, w2), (a1_in, a1))
        )
    ]
    height, _, lon = source.shape
    wide = columns.shape[3]
    ends = (0, height - 4), (0, height - 2)
    loads, saves = [], []
    for k, (residual, middle, target) in enumerate(((source, hid, out), (upstream, inn, grad))):
        for j in range(2):
            loads.append(
                pltpu.make_async_copy(
                    middle.at[pl.ds(ends[0][j], 4)], mid.at[2 * k + j], sem.at[0, 2 * k + j]
                )
            )
            loads.append(
                pltpu.make_async_copy(
                    residual.at[pl.ds(ends[1][j], 2)], res.at[2 * k + j], sem.at[1, 2 * k + j]
                )
            )
            saves.append(
                pltpu.make_async_copy(
                    result.at[2 * k + j], target.at[pl.ds(ends[1][j], 2)], sem.at[2, 2 * k + j]
                )
            )
    start(firsts[:2] + loads[0:8:2] + firsts[2:] + loads[1:8:2])
    wait(firsts[:2] + loads[0:8:2])
    for k in range(2):
        for r in range(2):
            store_row(columns.at[2 * k], r, above[2 * k + r][:, :lon])
            store_row(columns.at[2 * k + 1], 4 + r, below[2 * k + r][:, :lon])
    wait(firsts[2:] + loads[1:8:2])
    for k, weight in enumerate((w2, a1)):
        for j in range(2):
            for r in range(4):
                store_row(columns.at[2 * k + j], r + 2 - 2 * j, mid[2 * k + j, r][:, :lon])
        rhs = jnp.concatenate(
            [taps_of(columns.at[2 * k + j], r) for j in range(2) for r in range(2)], axis=1
        )
        value = jnp.dot(weight[...], rhs, preferred_element_type=F32)
        for j in range(2):
            for r in range(2):
                lo = (2 * j + r) * wide
                part = value[:, lo : lo + lon]
                base = res[2 * k + j, r].astype(F32)
                result[2 * k + j, r] = (base + part).astype(BF16)
    start(saves)
    wait(saves)


def column_body(got, after, mine, *gives):
    del after
    me = lax.axis_index("fsdp")

    def total(f):
        value = got[0, f].astype(F32)
        for i in range(1, got.shape[0]):
            value += got[i, f].astype(F32)
        return value

    mine[...] = total(me)
    for d, give in enumerate(gives):
        give[...] = total(me ^ (d + 1)).astype(BF16)


def chunk_body(mine, *refs):
    total = mine[...]
    for piece in refs[:-1]:
        total += piece[...].astype(F32)
    for band in range(refs[-1].shape[0]):
        refs[-1][band] = total


def unpack_body(share, depth, chunks, one, two):
    for k, result in enumerate((one, two)):

        def slab(s):
            parts = []
            start = s * share
            while start < (s + 1) * share:
                chunk, inside = divmod(start, depth)
                stop = min((s + 1) * share, (chunk + 1) * depth)
                lo = k * depth + inside
                parts.append(chunks[chunk, lo : lo + stop - start])
                start = stop
            return parts[0] if len(parts) == 1 else jnp.concatenate(parts, axis=0)

        for tap in range(TAPS):
            result[tap] = from_slabs(slab, tap)


def per_device(fields, cotangent, kernel_one, kernel_two):
    _, height, lon, c = fields.shape
    share = kernel_one.shape[3]
    shards = lax.axis_size("fsdp")
    bands = lax.axis_size("lat")
    wide = -(-lon // LANES) * LANES
    scale = 1.0 / (shards * fields.shape[0] * bands * height * lon) ** 0.5
    source = jnp.swapaxes(fields[0], 1, 2)
    upstream = jnp.swapaxes(cotangent[0], 1, 2)
    small = [
        jnp.swapaxes(k.reshape(TAPS, c, share), 1, 2) for k in (kernel_one, kernel_two)
    ]
    forward = [(i, i + 1) for i in range(bands - 1)]
    backward = [(i + 1, i) for i in range(bands - 1)]
    swap = [(i, i ^ 1) for i in range(bands)]

    def edges(top, bottom):
        return lax.ppermute(bottom, "lat", forward), lax.ppermute(top, "lat", backward)

    def partner(value, d):
        return lax.ppermute(value, "fsdp", [(i, i ^ d) for i in range(shards)])

    conv_flops = 2 * TAPS * c * c * height * lon
    groups = height // GROUP
    depth = -(-SLABS * share // (8 * bands)) * 8
    others = range(1, shards)
    slabs = shape(2 * HALF, share, LANES)
    half, rest, top, bottom = call(
        pack_body,
        "pack",
        [
            (slabs, VMEM),
            (slabs, VMEM),
            (shape(4, c, lon), VMEM),
            (shape(4, c, lon), VMEM),
        ],
        [ANY] * 4,
        (*small, source, upstream),
        scratch=[pltpu.VMEM((TAPS, share, c), BF16)] * 2 + [pltpu.SemaphoreType.DMA((6,))],
        limit=60,
    )
    pieces = [partner(half, d) for d in others]
    above, below = edges(top, bottom)
    pieces = pl.pallas_call(
        gate_body,
        name="gate",
        out_shape=[slabs for _ in others],
        in_specs=[VMEM] * (shards + 1),
        out_specs=[VMEM for _ in others],
        input_output_aliases={i: i for i in range(shards - 1)},
        compiler_params=pltpu.CompilerParams(vmem_limit_bytes=16 << 20),
    )(*pieces, above, below)
    swapped = [lax.ppermute(piece, "lat", swap) for piece in pieces]
    kernels = (half, *pieces, rest, *swapped)

    middle = shape(height, c, wide)
    edge = shape(4, c, wide)
    plain = pltpu.VMEM((height, c, lon), BF16)
    lined = pltpu.VMEM((height, c, wide), BF16)
    columns = pltpu.VMEM((height + 4, 3 * c, wide), BF16)
    matrix = pltpu.VMEM((c, TAPS * c), BF16)
    total = pltpu.VMEM((TAPS * c, c), F32)
    halo = pltpu.VMEM((4, c, lon), BF16)
    gathered = pltpu.VMEM((shards, *slabs.shape), BF16)
    piece_sems = pltpu.SemaphoreType.DMA((2 * shards,))
    hid, inn, top, bottom, terms = call(
        functools.partial(stage_body, scale, shards),
        "stage",
        [
            (middle, ANY),
            (middle, ANY),
            (edge, ANY),
            (edge, ANY),
            (shape(bands, shards, 2 * depth, LANES), VMEM),
        ],
        [ANY] * (4 + 2 * shards),
        (source, upstream, above, below, *kernels),
        scratch=[plain, plain, columns, columns, matrix, matrix, lined, lined, total, total]
        + [halo, halo, gathered, gathered]
        + [pltpu.SemaphoreType.DMA((4, groups)), pltpu.SemaphoreType.DMA((6,)), piece_sems],
        limit=60,
        flops=4 * conv_flops,
        nbytes=1 << 24,
    )
    above, below = edges(top, bottom)
    got = lax.all_to_all(terms, "lat", 0, 0, tiled=True)
    columns = pltpu.VMEM((height, 3 * c, wide), BF16)
    outs = (shape(height, c, lon), ANY)
    weight = (shape(c, TAPS * c), ANY)
    out, grad, w2, a1, token = call(
        functools.partial(interior_body, shards),
        "interior",
        [outs, outs, weight, weight, (shape(8, LANES, dtype=F32), VMEM)],
        [ANY] * (4 + 2 * shards),
        (source, upstream, hid, inn, *kernels),
        scratch=[plain, plain, lined, lined, columns, columns, plain, plain]
        + [matrix, matrix, gathered, gathered]
        + [pltpu.SemaphoreType.DMA((6, groups)), pltpu.SemaphoreType.DMA((2,)), piece_sems],
        limit=60,
        flops=2 * conv_flops,
        nbytes=1 << 24,
    )
    mine, *gives = call(
        column_body,
        "column",
        [(shape(2 * depth, LANES, dtype=F32), VMEM)]
        + [(shape(2 * depth, LANES), VMEM) for _ in others],
        [VMEM, VMEM],
        (got, token),
    )
    gains = [partner(give, d) for d, give in zip(others, gives)]
    (chunk,) = call(
        chunk_body,
        "chunk",
        [(shape(bands, 2 * depth, LANES, dtype=F32), VMEM)],
        [VMEM] * shards,
        (mine, *gains),
    )
    chunks = lax.all_to_all(chunk, "lat", 0, 0, tiled=True)
    out, grad = pl.pallas_call(
        edge_body,
        name="edge",
        out_shape=[outs[0], outs[0]],
        in_specs=[ANY] * 10,
        out_specs=[ANY, ANY],
        input_output_aliases={8: 0, 9: 1},
        scratch_shapes=[
            pltpu.VMEM((4, 2, c, lon), BF16),
            pltpu.VMEM((4, 4, c, wide), BF16),
            pltpu.VMEM((4, 6, 3 * c, wide), BF16),
            pltpu.VMEM((4, 2, c, lon), BF16),
            pltpu.VMEM(edge.shape, BF16),
            pltpu.VMEM(edge.shape, BF16),
            matrix,
            matrix,
            pltpu.SemaphoreType.DMA((4, 4)),
        ],
        compiler_params=pltpu.CompilerParams(vmem_limit_bytes=60 << 20),
        cost_estimate=pl.CostEstimate(
            flops=conv_flops // 2, bytes_accessed=1 << 22, transcendentals=0
        ),
    )(source, upstream, hid, inn, above, below, w2, a1, out, grad)
    one, two = call(
        functools.partial(unpack_body, share, depth),
        "unpack",
        [(shape(TAPS, share, c, dtype=F32), VMEM)] * 2,
        [VMEM],
        (chunks,),
    )
    return (
        jnp.swapaxes(out, 1, 2)[None],
        jnp.swapaxes(grad, 1, 2)[None],
        jnp.swapaxes(one, 1, 2).reshape(3, 3, c, share),
        jnp.swapaxes(two, 1, 2).reshape(3, 3, c, share),
    )


def solution(mesh):
    placed = (
        P("fsdp", "lat", None, None),
        P("fsdp", "lat", None, None),
        P(None, None, None, "fsdp"),
        P(None, None, None, "fsdp"),
    )
    return jax.shard_map(
        per_device,
        mesh=mesh,
        in_specs=placed,
        out_specs=placed,
        check_vma=False,
    )
```
